256 devices in a mesh: row: 8 (over x, z_lo), col: 32 (over y, z_hi, core).
Axes of the slice: x: 4, y: 4, z: 8 (z_hi: 4, z_lo: 2; z = z_hi * 2 + z_lo), core: 2. Of those that a mesh axis runs over, the one named last changes fastest.
Arguments:
- state_cov: float32 [8192, 8192], P('row', 'col'), may hold values from -6 to 6
- trans_first: float32 [64, 9, 128, 128], P('row'), may hold values from -0.1875 to 0.1875
- band_first: int32 [64, 9], P('row'), may hold values from 0 to 63, as said below
- trans_second: float32 [64, 9, 128, 128], P('col'), may hold values from -0.1875 to 0.1875
- band_second: int32 [64, 9], P('col'), may hold values from 0 to 63, as said below
- noise_cov: float32 [8192, 8192], P('col', 'row'), may hold values from -4 to 4
Outputs:
- forecast: float32 [8192, 8192], P('col', 'row')
The draws below stay inside these ranges and needn't reach their ends.
Inputs may be any that keep to these rules, and one draw needn't show every extreme that they name: `band_first`: row i lists 9 different block columns in increasing order, each within 8 of i; block rows 0 and 63 reach exactly 8 blocks away. `band_second`: row i lists 9 different block columns in increasing order, each within 8 of i; block rows 0 and 63 reach exactly 8 blocks away.
All inputs are finite; a program needn't handle non-finite values.
Results may differ from the reference program's by a relative error of at most 0.0003.
Values sent between devices are 32-bit elements; how exact they have to be, the bound alone decides.
A program may use at most 128 MiB of HBM per device.

```python
import jax
import jax.numpy as jnp
from jax import lax

N = 8192
BS = 128
BAND = 9
REACH = 8
BLOCKS = 64


def band_table(key):
    window = 2 * REACH + 1
    ranking = jax.random.randint(key, (BLOCKS, window), 0, 1 << 20) * window + jnp.arange(window, dtype=jnp.int32)[None, :]
    position = jnp.arange(BLOCKS, dtype=jnp.int32)[:, None] - REACH + jnp.arange(window, dtype=jnp.int32)[None, :]
    inside = (position >= 0) & (position < BLOCKS)
    ranking = jnp.where(inside, ranking, -1)
    unused, chosen = lax.top_k(ranking, BAND)
    picked = jnp.take_along_axis(position, chosen, axis=1)
    return jnp.sort(picked, axis=1).astype(jnp.int32)


def draw_band_first(key, part):
    return band_table(jax.random.fold_in(key, 11))


def draw_band_second(key, part):
    return band_table(jax.random.fold_in(key, 23))


def steps_of(rng, dims, cuts, low, largest):
    gain, own = 1.0, jax.random.fold_in(rng, 6)
    for axis_at, shards_of in cuts:
        draws = jnp.exp(jax.random.uniform(jax.random.fold_in(own, axis_at), (shards_of,), jnp.float32, low / len(cuts), largest / len(cuts)))
        gain = gain * jnp.repeat(draws, dims[axis_at] // shards_of).reshape([-1 if axis == axis_at else 1 for axis in range(len(dims))])
    return gain


def centred(key, shape, width, reach, split=(), kind=jnp.bfloat16):
    factor_of = steps_of(key, shape, split, -0.22, 0.18) if split else 1.0
    values = jax.random.normal(key, shape, jnp.float32) * width * factor_of
    return jnp.minimum(jnp.maximum(values, -reach), reach).astype(kind)


def setup_inputs(seed: int = 0) -> dict:
    seeds = jax.random.split(jax.random.key(seed), 7)
    state_cov = centred(seeds[0], (N, N), 1.0, 6.0, ((0, 8), (1, 32)), jnp.float32)
    trans_first = centred(seeds[1], (BLOCKS, BAND, BS, BS), (BAND * BS) ** -0.5, 0.1875, ((0, 8),), jnp.float32)
    band_first = draw_band_first(jax.random.fold_in(seeds[6], 71), 0)
    trans_second = centred(seeds[3], (BLOCKS, BAND, BS, BS), (BAND * BS) ** -0.5, 0.1875, ((0, 32),), jnp.float32)
    band_second = draw_band_second(jax.random.fold_in(seeds[6], 71), 0)
    noise_cov = centred(seeds[5], (N, N), 0.5, 4.0, ((0, 32), (1, 8)), jnp.float32)
    return dict(state_cov=state_cov, trans_first=trans_first, band_first=band_first, trans_second=trans_second, band_second=band_second, noise_cov=noise_cov)


def band_product(blocks, offsets, field):
    block_tiles = field.reshape(BLOCKS, BS, field.shape[1])

    def single(pair):
        matrix_rows, columns = pair
        picked = jnp.take(block_tiles, columns.astype(jnp.int32), axis=0)
        return jnp.einsum("tik,tkc->ic", matrix_rows, picked, precision=lax.Precision.HIGHEST)

    result = lax.map(single, (blocks, offsets))
    return result.reshape(N, field.shape[1])


def reference(state_cov, trans_first, band_first, trans_second, band_second, noise_cov):
    advected = band_product(trans_first, band_first, state_cov)
    return band_product(trans_second, band_second, advected.T) + noise_cov
```

```python
import jax
import jax.numpy as jnp
from jax import lax
from jax.experimental import pallas as pl
from jax.experimental.pallas import tpu as pltpu
from jax.sharding import PartitionSpec as P

BAND = 9
REACH = 8
BS = 128
MESH = pl.DeviceIdType.MESH


def halves(x):
    high = x.astype(jnp.bfloat16)
    low = (x - high.astype(jnp.float32)).astype(jnp.bfloat16)
    return high, low


def dot(a, b):
    return jnp.dot(a, b, preferred_element_type=jnp.float32)


def kernel(
    rows, cols,
    band1, band2, s_ref, a1_ref, a2_ref, out_ref,
    hb, hbh, hbl, a1f, ah, a2f, wh, wl, rx, acc,
    own_send, direct_recv, far_send, far_recv, tile_send, tile_recv, local_sem,
):
    r = lax.axis_index("row")
    c = lax.axis_index("col")
    p = r % 2
    core = c % 2
    mate = r + 1 - 2 * p
    other = c + 1 - 2 * core
    far_to = r + 2 - 4 * p
    far_from = r - 2 + 4 * p
    has_far_to = jnp.logical_and(far_to >= 0, far_to < rows)
    has_far_from = jnp.logical_and(far_from >= 0, far_from < rows)
    left1, right1 = c >= 2, c + 2 < cols
    left2, right2 = c >= 4, c + 4 < cols
    both = jnp.logical_and(left1, right1)
    far_share = jnp.logical_or(
        jnp.logical_and(core == 0, right2), jnp.logical_and(core == 1, left2)
    )

    load_own = pltpu.make_async_copy(s_ref, hb.at[pl.ds(8, 8)], local_sem.at[0])
    load_a1 = pltpu.make_async_copy(a1_ref, a1f, local_sem.at[1])
    load_a2 = pltpu.make_async_copy(a2_ref, a2f, local_sem.at[2])
    load_own.start()
    load_a2.start()
    load_a1.start()

    barrier = pltpu.get_barrier_semaphore()
    neighbours = (
        (None, (mate, c)),
        (None, (r, other)),
        (left1, (r, c - 2)),
        (right1, (r, c + 2)),
        (r >= 2, (r - 2, c)),
        (r + 2 < rows, (r + 2, c)),
    )
    for cond, device in neighbours:
        def greet(device=device):
            pl.semaphore_signal(barrier, inc=1, device_id=device, device_id_type=MESH)
        greet() if cond is None else pl.when(cond)(greet)
    peers = jnp.int32(0)
    for cond, _ in neighbours:
        peers = peers + (1 if cond is None else cond.astype(jnp.int32))
    pl.semaphore_wait(barrier, peers)

    def remote(src, dst, send, recv, device):
        return pltpu.make_async_remote_copy(
            src_ref=src, dst_ref=dst, send_sem=send, recv_sem=recv,
            device_id=device, device_id_type=MESH,
        )

    near_at = 16 - 16 * p
    away_at = 16 * p

    def send_own(k):
        return remote(s_ref.at[k], hb.at[16 * p + k], own_send.at[k], direct_recv.at[k], (mate, c))

    def got_direct(k):
        return remote(s_ref.at[k], hb.at[near_at + k], own_send.at[k], direct_recv.at[k], (mate, c))

    def send_far(k):
        return remote(hb.at[near_at + k], hb.at[16 * p + k], far_send.at[k], far_recv.at[k], (far_to, c))

    def got_far(k):
        return remote(hb.at[near_at + k], hb.at[away_at + k], far_send.at[k], far_recv.at[k], (mate, c))

    def each(n, body):
        def step(k, carry):
            body(k)
            return carry
        lax.fori_loop(0, n, step, 0)

    each(8, lambda k: send_own(k).start())
    load_own.wait()
    load_a2.wait()
    load_a1.wait()

    def build_w(d):
        for j in range(2):
            for kk in range(2):
                block = 2 * c - REACH + 2 * d + kk
                slot = jnp.int32(0)
                there = jnp.int32(0)
                for t in range(BAND):
                    hit = (band2[j, t] == block).astype(jnp.int32)
                    slot = slot + t * hit
                    there = there + hit
                m = (a2f[j, jnp.minimum(slot, BAND - 1)] * there.astype(jnp.float32)).T
                h, l = halves(m)
                wh[d, kk * BS:(kk + 1) * BS, j * BS:(j + 1) * BS] = h
                wl[d, kk * BS:(kk + 1) * BS, j * BS:(j + 1) * BS] = l

    def split_rows(at):
        h, l = halves(hb[at])
        hbh[at] = h
        hbl[at] = l

    def halo_step(k):
        for t in range(BAND):
            h, l = halves(a1f[k, t])
            ah[k, 0:BS, t * BS:(t + 1) * BS] = h
            ah[k, BS:2 * BS, t * BS:(t + 1) * BS] = l
        build_w(k)
        split_rows(8 + k)
        got_direct(k).wait_recv()

        @pl.when(has_far_to)
        def _():
            send_far(k).start()

        split_rows(near_at + k)

    each(8, halo_step)
    build_w(8)

    @pl.when(has_far_from)
    def _():
        def step(k):
            got_far(k).wait_recv()
            split_rows(away_at + k)
        each(8, step)

    RIGHT, LEFT, SHARE, FWD_RIGHT, FWD_LEFT, SHARE_L, SHARE_R, SHARE_FAR = range(8)

    def tile_copy(kind, i):
        src, dst, device = {
            RIGHT: (4, 2, (r, c + 2)),
            LEFT: (4, 6, (r, c - 2)),
            SHARE: (4, 3 + 2 * core, (r, other)),
            FWD_RIGHT: (2, 0, (r, c + 2)),
            FWD_LEFT: (6, 8, (r, c - 2)),
            SHARE_L: (2, 1 + 2 * core, (r, other)),
            SHARE_R: (6, 5 + 2 * core, (r, other)),
            SHARE_FAR: (8 - 8 * core, 7 - 6 * core, (r, other)),
        }[kind]
        return remote(rx.at[src, i], rx.at[dst, i], tile_send.at[kind, i], tile_recv.at[dst, i], device)

    def got_tile(slot, i):
        return remote(rx.at[4, i], rx.at[slot, i], tile_send.at[0, i], tile_recv.at[slot, i], (r, other))

    def add_tile(slot, i, first=False):
        h, l = halves(rx[slot, i])
        top = dot(jnp.concatenate([h, l], axis=0), wh[slot])
        total = top[:BS] + top[BS:] + dot(h, wl[slot])
        if first:
            acc[i] = total
        else:
            acc[i] += total

    def advect(i):
        ids = [jnp.clip(band1[i, t] - 8 * r + REACH, 0, 23) for t in range(BAND)]
        xh = jnp.concatenate([hbh[k] for k in ids], axis=0)
        xl = jnp.concatenate([hbl[k] for k in ids], axis=0)
        top = dot(ah[i], xh)
        rx[4, i] = top[:BS] + top[BS:] + dot(ah[i, 0:BS], xl)

        @pl.when(right1)
        def _():
            tile_copy(RIGHT, i).start()

        @pl.when(left1)
        def _():
            tile_copy(LEFT, i).start()

        tile_copy(SHARE, i).start()

    each(8, advect)

    each(8, lambda i: add_tile(4, i, first=True))

    def near_step(i):
        got_tile(5 - 2 * core, i).wait_recv()
        add_tile(5 - 2 * core, i)

        @pl.when(left1)
        def _():
            got_tile(2, i).wait_recv()
            tile_copy(SHARE_L, i).start()

            @pl.when(right1)
            def _():
                tile_copy(FWD_RIGHT, i).start()

            add_tile(2, i)

        @pl.when(right1)
        def _():
            got_tile(6, i).wait_recv()
            tile_copy(SHARE_R, i).start()

            @pl.when(left1)
            def _():
                tile_copy(FWD_LEFT, i).start()

            add_tile(6, i)

    each(8, near_step)

    def mid_step(i):
        @pl.when(left1)
        def _():
            got_tile(3 - 2 * core, i).wait_recv()
            add_tile(3 - 2 * core, i)

        @pl.when(right1)
        def _():
            got_tile(7 - 2 * core, i).wait_recv()
            add_tile(7 - 2 * core, i)

    each(8, mid_step)

    def far_step(i):
        @pl.when(left2)
        def _():
            got_tile(0, i).wait_recv()

        @pl.when(right2)
        def _():
            got_tile(8, i).wait_recv()

        @pl.when(far_share)
        def _():
            tile_copy(SHARE_FAR, i).start()

        @pl.when(left2)
        def _():
            add_tile(0, i)

        @pl.when(right2)
        def _():
            add_tile(8, i)

        @pl.when(jnp.logical_or(
            jnp.logical_and(core == 0, left2), jnp.logical_and(core == 1, right2)
        ))
        def _():
            got_tile(1 + 6 * core, i).wait_recv()
            add_tile(1 + 6 * core, i)

        out_ref[:, pl.ds(pl.multiple_of(i * BS, BS), BS)] = acc[i].T

    each(8, far_step)

    def drain(i):
        send_own(i).wait_send()
        tile_copy(SHARE, i).wait_send()

        @pl.when(has_far_to)
        def _():
            send_far(i).wait_send()

        @pl.when(right1)
        def _():
            tile_copy(RIGHT, i).wait_send()
            tile_copy(SHARE_R, i).wait_send()

        @pl.when(left1)
        def _():
            tile_copy(LEFT, i).wait_send()
            tile_copy(SHARE_L, i).wait_send()

        @pl.when(both)
        def _():
            tile_copy(FWD_RIGHT, i).wait_send()
            tile_copy(FWD_LEFT, i).wait_send()

        @pl.when(far_share)
        def _():
            tile_copy(SHARE_FAR, i).wait_send()

    each(8, drain)


def solution(mesh):
    rows, cols = mesh.shape["row"], mesh.shape["col"]

    def body(state_cov, trans_first, band_first, trans_second, band_second, noise_cov):
        width = state_cov.shape[1]
        tiles = state_cov.reshape(8, BS, width)
        f32, bf16 = jnp.float32, jnp.bfloat16
        smem = pl.BlockSpec(memory_space=pltpu.SMEM)
        anyspace = pl.BlockSpec(memory_space=pl.ANY)
        product = pl.pallas_call(
            lambda *refs: kernel(rows, cols, *refs),
            out_shape=jax.ShapeDtypeStruct((width, 8 * BS), f32),
            in_specs=[smem, smem, anyspace, anyspace, anyspace],
            out_specs=pl.BlockSpec(memory_space=pltpu.VMEM),
            scratch_shapes=[
                pltpu.VMEM((24, BS, width), f32),
                pltpu.VMEM((24, BS, width), bf16),
                pltpu.VMEM((24, BS, width), bf16),
                pltpu.VMEM((8, BAND, BS, BS), f32),
                pltpu.VMEM((8, 2 * BS, BAND * BS), bf16),
                pltpu.VMEM((2, BAND, BS, BS), f32),
                pltpu.VMEM((9, width, width), bf16),
                pltpu.VMEM((9, width, width), bf16),
                pltpu.VMEM((9, 8, BS, width), f32),
                pltpu.VMEM((8, BS, width), f32),
                pltpu.SemaphoreType.DMA((8,)),
                pltpu.SemaphoreType.DMA((8,)),
                pltpu.SemaphoreType.DMA((8,)),
                pltpu.SemaphoreType.DMA((8,)),
                pltpu.SemaphoreType.DMA((8, 8)),
                pltpu.SemaphoreType.DMA((9, 8)),
                pltpu.SemaphoreType.DMA((3,)),
            ],
            compiler_params=pltpu.CompilerParams(
                collective_id=0, has_side_effects=True, vmem_limit_bytes=60 * 2**20
            ),
            name="forecast",
        )(band_first, band_second, tiles, trans_first, trans_second)
        return product + noise_cov

    return jax.shard_map(
        body,
        mesh=mesh,
        in_specs=(
            P("row", "col"),
            P("row", None, None, None),
            P("row", None),
            P("col", None, None, None),
            P("col", None),
            P("col", "row"),
        ),
        out_specs=P("col", "row"),
        check_vma=False,
    )
```

```python
import jax
import jax.numpy as jnp
from jax import lax
from jax.experimental import pallas as pl
from jax.experimental.pallas import tpu as pltpu
from jax.sharding import PartitionSpec as P

BAND = 9
REACH = 8
BS = 128
MESH = pl.DeviceIdType.MESH


def halves(x):
    high = x.astype(jnp.bfloat16)
    low = (x - high.astype(jnp.float32)).astype(jnp.bfloat16)
    return high, low


def dot(a, b):
    return jnp.dot(a, b, preferred_element_type=jnp.float32)


def product(a, xs_high, xs_low):
    top = dot(a, jnp.concatenate(xs_high, axis=0))
    return top[:BS] + top[BS:] + dot(a[:BS], jnp.concatenate(xs_low, axis=0))


def each(n, body):
    def step(k, carry):
        body(k)
        return carry
    lax.fori_loop(0, n, step, 0)


def remote(src, dst, send, recv, device):
    return pltpu.make_async_remote_copy(
        src_ref=src, dst_ref=dst, send_sem=send, recv_sem=recv,
        device_id=device, device_id_type=MESH,
    )


def both(*conds):
    out = conds[0]
    for cond in conds[1:]:
        out = jnp.logical_and(out, cond)
    return out


def either(*conds):
    out = conds[0]
    for cond in conds[1:]:
        out = jnp.logical_or(out, cond)
    return out


def kernel(
    rows, cols,
    band1, band2, s_ref, a1_ref, a2_ref, out_ref,
    hb, hbh, hbl, a1f, a1s, a2f, a2s, stage, g0, g1, gh, gl, res, resin, band_mine, band_all, bands,
    own_send, direct_recv, far_send, far_recv,
    slab_send, slab_recv, chain_send, wide_send, wide_recv,
    band_send, band_recv, in_send, in_recv, share_send, share_recv, side_send, side_recv,
    back_send, back_recv, local_sem,
):
    r = lax.axis_index("row")
    c = lax.axis_index("col")
    y = c // 8
    q = c % 8
    h = q // 2
    core = q % 2
    owner = h // 2
    mine = q % 4
    base = 8 * y + 4 * core
    local_owner = core == owner
    x = r // 2
    p = r % 2
    mate = r + 1 - 2 * p
    other = c + 1 - 2 * core
    far_to = r + 2 - 4 * p
    far_from = r - 2 + 4 * p
    has_far_to = both(far_to >= 0, far_to < rows)
    has_far_from = both(far_from >= 0, far_from < rows)
    side = c - 7 + 14 * core
    has_side = both(side >= 0, side < cols)
    out_row = r + 1 - 2 * p
    out_h = (h + 3 + 2 * p) % 4

    load_own = pltpu.make_async_copy(s_ref, hb.at[pl.ds(8, 8)], local_sem.at[0])
    load_a1 = pltpu.make_async_copy(a1_ref, a1f, local_sem.at[1])
    load_a2 = pltpu.make_async_copy(a2_ref, a2f.at[mine], local_sem.at[2])
    load_own.start()
    load_a1.start()

    @pl.when(local_owner)
    def _():
        load_a2.start()

    barrier = pltpu.get_barrier_semaphore()

    def greet(device):
        pl.semaphore_signal(barrier, inc=1, device_id=device, device_id_type=MESH)

    for o in range(1, 8):
        greet((r, 8 * y + (q + o) % 8))
    for o in range(1, rows // 2):
        greet(((r + 2 * o) % rows, c))
    for k in range(2):
        greet((mate, 8 * y + 2 * h + k))
        greet((out_row, 8 * y + 2 * out_h + k))

    @pl.when(has_side)
    def _():
        greet((r, side))

    pl.semaphore_wait(barrier, 7 + rows // 2 - 1 + 4 + has_side.astype(jnp.int32))

    near_at = 16 - 16 * p
    away_at = 16 * p

    def send_own(k):
        return remote(s_ref.at[k], hb.at[16 * p + k], own_send.at[k], direct_recv.at[k], (mate, c))

    def got_direct(k):
        return remote(s_ref.at[k], hb.at[near_at + k], own_send.at[k], direct_recv.at[k], (mate, c))

    def send_far(k):
        return remote(hb.at[near_at + k], hb.at[16 * p + k], far_send.at[k], far_recv.at[k], (far_to, c))

    def got_far(k):
        return remote(hb.at[near_at + k], hb.at[away_at + k], far_send.at[k], far_recv.at[k], (mate, c))

    each(8, lambda k: send_own(k).start())

    part = BS // (rows // 2)

    def piece(m, at):
        return a2f.at[m, :, :, pl.ds(pl.multiple_of(part * at, part), part), :]

    slab_to_mate_core = remote(a2_ref, a2f.at[mine], slab_send.at[0], slab_recv.at[mine], (r, other))
    slab_out = remote(
        a2_ref.at[:, :, pl.ds(pl.multiple_of(part * x, part), part), :], piece(mine, x),
        slab_send.at[1], slab_recv.at[mine], (out_row, 8 * y + 2 * out_h + owner),
    )
    slab_out.start()

    @pl.when(jnp.logical_not(local_owner))
    def _():
        slab_to_mate_core.start()

    def far_of(m):
        return (2 * core + m // 2 - h + 4) % 4

    def chain_conds(m):
        d = far_of(m)
        first = m % 2 == 0
        to_mate = either(
            both(d == 3, p == 0), both(d == 1, p == 1),
            both(d == 2, first, p == 0), both(d == 2, jnp.logical_not(first), p == 1),
        )
        to_out = either(both(d == 3, p == 1, first), both(d == 1, p == 0, jnp.logical_not(first)))
        return d, to_mate, to_out

    def chain_copy(m, way):
        device = (mate, c) if way == 0 else (out_row, 8 * y + 2 * out_h + core)
        return remote(piece(m, x), piece(m, x), chain_send.at[m, way], slab_recv.at[m], device)

    def wide_copy(m, o):
        return remote(piece(m, x), piece(m, x), wide_send.at[m, o - 1], wide_recv.at[m, o - 1], ((r + 2 * o) % rows, c))

    def got_wide(m, o):
        at = (x - o + rows // 2) % (rows // 2)
        return remote(piece(m, x), piece(m, at), wide_send.at[m, o - 1], wide_recv.at[m, o - 1], (mate, c))

    def chain_step(m, far):
        d, to_mate, to_out = chain_conds(m)

        @pl.when((d == 2) if far else (d % 2 == 1))
        def _():
            chain_copy(m, 0).wait_recv()

            @pl.when(to_mate)
            def _():
                chain_copy(m, 0).start()

            @pl.when(to_out)
            def _():
                chain_copy(m, 1).start()

            for o in range(1, rows // 2):
                wide_copy(m, o).start()

    row_id = lax.broadcasted_iota(jnp.int32, (8, BS), 0)
    lane_id = lax.broadcasted_iota(jnp.int32, (8, BS), 1)
    table = jnp.zeros((8, BS), jnp.int32)
    for j in range(2):
        for t in range(BAND):
            table = jnp.where(both(row_id == j, lane_id == t), band2[j, t], table)
    band_mine[...] = table

    @pl.when(local_owner)
    def _():
        band_all[mine] = table

    def group_copy(src, dst, send, recv, o):
        return remote(src, dst, send, recv, (r, 8 * y + 2 * ((h + o) % 4) + owner))

    def band_copy(o):
        return group_copy(band_mine, band_all.at[mine], band_send.at[o], band_recv.at[mine], o)

    def got_band(m):
        return remote(band_mine, band_all.at[m], band_send.at[0], band_recv.at[m], (mate, c))

    def is_remote(o):
        return jnp.logical_or(o != 0, jnp.logical_not(local_owner))

    for o in range(4):
        @pl.when(is_remote(o))
        def _():
            band_copy(o).start()

    load_own.wait()
    load_a1.wait()

    def split_rows(at):
        high, low = halves(hb[at])
        hbh[at] = high
        hbl[at] = low

    def halo_step(k):
        for t in range(BAND):
            high, low = halves(a1f[k, t])
            a1s[k, 0:BS, t * BS:(t + 1) * BS] = high
            a1s[k, BS:2 * BS, t * BS:(t + 1) * BS] = low
        split_rows(8 + k)
        got_direct(k).wait_recv()

        @pl.when(has_far_to)
        def _():
            send_far(k).start()

        split_rows(near_at + k)

    each(4, halo_step)
    each(4, lambda m: chain_step(m, False))
    each(4, lambda k: halo_step(4 + k))
    each(4, lambda m: chain_step(m, True))

    @pl.when(has_far_from)
    def _():
        def step(k):
            got_far(k).wait_recv()
            split_rows(away_at + k)
        each(8, step)

    gs = (g0, g1)

    def in_copy(e, o):
        hp = (h + o) % 4
        return group_copy(stage.at[e, hp], gs[e].at[pl.ds(8 + 2 * mine, 2)], in_send.at[e, o], in_recv.at[e, mine], o)

    def got_in(e, m):
        return remote(stage.at[e, 0], gs[e].at[pl.ds(8 + 2 * m, 2)], in_send.at[e, 0], in_recv.at[e, m], (mate, c))

    for e in range(2):
        def advect(n, e=e):
            o = 3 - n
            hp = (h + o) % 4
            i = 2 * hp + e
            ids = [jnp.clip(band1[i, t] - 8 * r + REACH, 0, 23) for t in range(BAND)]
            tile = product(a1s[i], [hbh[k] for k in ids], [hbl[k] for k in ids])
            for b in range(2):
                stage[e, hp, b] = tile[:, b * BS:(b + 1) * BS].T

            @pl.when(is_remote(o))
            def _():
                in_copy(e, o).start()

            @pl.when(jnp.logical_not(is_remote(o)))
            def _():
                for b in range(2):
                    gs[e][8 + 2 * mine + b] = stage[e, hp, b]
        each(4, advect)

    for m in range(4):
        @pl.when(base + m != c)
        def _():
            got_band(m).wait_recv()
    to_scalars = pltpu.make_async_copy(band_all, bands, local_sem.at[3])
    to_scalars.start()

    def share_copy(e, m):
        return remote(
            gs[e].at[pl.ds(8 + 2 * m, 2)], gs[e].at[pl.ds(16 * core + 2 * m, 2)],
            share_send.at[e, m], share_recv.at[e, m], (r, other),
        )

    def side_copy(e, m):
        return remote(
            gs[e].at[pl.ds(8 + 2 * m, 2)], gs[e].at[pl.ds(16 - 16 * core + 2 * m, 2)],
            side_send.at[e, m], side_recv.at[e, m], (r, side),
        )

    def got_share(e, m):
        return remote(
            gs[e].at[pl.ds(8 + 2 * m, 2)], gs[e].at[pl.ds(16 - 16 * core + 2 * m, 2)],
            share_send.at[e, m], share_recv.at[e, m], (r, other),
        )

    def got_side(e, m):
        return remote(
            gs[e].at[pl.ds(8 + 2 * m, 2)], gs[e].at[pl.ds(16 * core + 2 * m, 2)],
            side_send.at[e, m], side_recv.at[e, m], (r, other),
        )

    def back_copy(e, m):
        return remote(res.at[e, m], resin.at[e, h], back_send.at[e, m], back_recv.at[e, h], (r, base + m))

    def got_back(e, hp):
        return remote(res.at[e, 0], resin.at[e, hp], back_send.at[e, 0], back_recv.at[e, hp], (mate, c))

    def split_pair(g, at):
        for b in range(2):
            high, low = halves(g[at + b])
            gh[at + b] = high
            gl[at + b] = low

    for e in range(2):
        def own_step(m, e=e):
            @pl.when(base + m != c)
            def _():
                got_in(e, m).wait_recv()

            share_copy(e, m).start()

            @pl.when(has_side)
            def _():
                side_copy(e, m).start()

            split_pair(gs[e], 8 + 2 * m)

        each(4, own_step)

        if e == 0:
            to_scalars.wait()

            @pl.when(local_owner)
            def _():
                load_a2.wait()

            def slab_step(m):
                @pl.when(both(far_of(m) == 0, base + m != c))
                def _():
                    remote(a2_ref, a2f.at[m], slab_send.at[0], slab_recv.at[m], (r, other)).wait_recv()

                @pl.when(far_of(m) != 0)
                def _():
                    for o in range(1, rows // 2):
                        got_wide(m, o).wait_recv()

                for jj in range(2):
                    for t in range(BAND):
                        high, low = halves(a2f[m, jj, t])
                        a2s[2 * m + jj, 0:BS, t * BS:(t + 1) * BS] = high
                        a2s[2 * m + jj, BS:2 * BS, t * BS:(t + 1) * BS] = low

            each(4, slab_step)

        def neighbour_step(m, e=e):
            got_share(e, m).wait_recv()
            split_pair(gs[e], 16 - 16 * core + 2 * m)

            @pl.when(has_side)
            def _():
                got_side(e, m).wait_recv()
                split_pair(gs[e], 16 * core + 2 * m)

        each(4, neighbour_step)

        def second(m, e=e):
            for jj in range(2):
                ids = [jnp.clip(bands[m, jj, t] - 2 * base + REACH, 0, 23) for t in range(BAND)]
                res[e, m, jj] = product(a2s[2 * m + jj], [gh[k] for k in ids], [gl[k] for k in ids])

            @pl.when(base + m != c)
            def _():
                back_copy(e, m).start()

        each(4, second)

    for e in range(2):
        def finish(hp, e=e):
            columns = pl.ds(pl.multiple_of((2 * hp + e) * BS, BS), BS)
            here = both(hp == h, local_owner)

            @pl.when(jnp.logical_not(here))
            def _():
                got_back(e, hp).wait_recv()
                for jj in range(2):
                    out_ref[jj * BS:(jj + 1) * BS, columns] = resin[e, hp, jj]

            @pl.when(here)
            def _():
                for jj in range(2):
                    out_ref[jj * BS:(jj + 1) * BS, columns] = res[e, mine, jj]

        each(4, finish)

    slab_out.wait_send()

    @pl.when(jnp.logical_not(local_owner))
    def _():
        slab_to_mate_core.wait_send()

    def drain_halo(k):
        send_own(k).wait_send()

        @pl.when(has_far_to)
        def _():
            send_far(k).wait_send()

    each(8, drain_halo)

    def drain(m):
        d, to_mate, to_out = chain_conds(m)

        @pl.when(d != 0)
        def _():
            @pl.when(to_mate)
            def _():
                chain_copy(m, 0).wait_send()

            @pl.when(to_out)
            def _():
                chain_copy(m, 1).wait_send()

            for o in range(1, rows // 2):
                wide_copy(m, o).wait_send()

        @pl.when(is_remote(m))
        def _():
            band_copy(m).wait_send()
            for e in range(2):
                in_copy(e, m).wait_send()

        for e in range(2):
            share_copy(e, m).wait_send()

            @pl.when(has_side)
            def _():
                side_copy(e, m).wait_send()

            @pl.when(base + m != c)
            def _():
                back_copy(e, m).wait_send()

    each(4, drain)


def solution(mesh):
    rows, cols = mesh.shape["row"], mesh.shape["col"]

    def body(state_cov, trans_first, band_first, trans_second, band_second, noise_cov):
        width = state_cov.shape[1]
        tiles = state_cov.reshape(8, BS, width)
        f32, bf16, i32 = jnp.float32, jnp.bfloat16, jnp.int32
        smem = pl.BlockSpec(memory_space=pltpu.SMEM)
        anyspace = pl.BlockSpec(memory_space=pl.ANY)
        dma = pltpu.SemaphoreType.DMA
        product_t = pl.pallas_call(
            lambda *refs: kernel(rows, cols, *refs),
            out_shape=jax.ShapeDtypeStruct((width, 8 * BS), f32),
            in_specs=[smem, smem, anyspace, anyspace, anyspace],
            out_specs=pl.BlockSpec(memory_space=pltpu.VMEM),
            scratch_shapes=[
                pltpu.VMEM((24, BS, width), f32),
                pltpu.VMEM((24, BS, width), bf16),
                pltpu.VMEM((24, BS, width), bf16),
                pltpu.VMEM((8, BAND, BS, BS), f32),
                pltpu.VMEM((8, 2 * BS, BAND * BS), bf16),
                pltpu.VMEM((4, 2, BAND, BS, BS), f32),
                pltpu.VMEM((8, 2 * BS, BAND * BS), bf16),
                pltpu.VMEM((2, 4, 2, BS, BS), f32),
                pltpu.VMEM((24, BS, BS), f32),
                pltpu.VMEM((24, BS, BS), f32),
                pltpu.VMEM((24, BS, BS), bf16),
                pltpu.VMEM((24, BS, BS), bf16),
                pltpu.VMEM((2, 4, 2, BS, BS), f32),
                pltpu.VMEM((2, 4, 2, BS, BS), f32),
                pltpu.VMEM((8, BS), i32),
                pltpu.VMEM((4, 8, BS), i32),
                pltpu.SMEM((4, 8, BS), i32),
                dma((8,)), dma((8,)), dma((8,)), dma((8,)),
                dma((2,)), dma((4,)), dma((4, 2)), dma((4, 3)), dma((4, 3)),
                dma((4,)), dma((4,)), dma((2, 4)), dma((2, 4)),
                dma((2, 4)), dma((2, 4)), dma((2, 4)), dma((2, 4)),
                dma((2, 4)), dma((2, 4)), dma((4,)),
            ],
            compiler_params=pltpu.CompilerParams(
                collective_id=0, has_side_effects=True, vmem_limit_bytes=60 * 2**20
            ),
            name="forecast",
        )(band_first, band_second, tiles, trans_first, trans_second)
        return product_t + noise_cov

    return jax.shard_map(
        body,
        mesh=mesh,
        in_specs=(
            P("row", "col"),
            P("row", None, None, None),
            P("row", None),
            P("col", None, None, None),
            P("col", None),
            P("col", "row"),
        ),
        out_specs=P("col", "row"),
        check_vma=False,
    )
```

```python
import jax
import jax.numpy as jnp
from jax import lax
from jax.experimental import pallas as pl
from jax.experimental.pallas import tpu as pltpu
from jax.sharding import PartitionSpec as P

BAND = 9
REACH = 8
BS = 128
MESH = pl.DeviceIdType.MESH


def halves(x):
    high = x.astype(jnp.bfloat16)
    low = (x - high.astype(jnp.float32)).astype(jnp.bfloat16)
    return high, low


def dot(a, b):
    return jnp.dot(a, b, preferred_element_type=jnp.float32)


def product(a, xs_high, xs_low):
    top = dot(a, jnp.concatenate(xs_high, axis=0))
    return top[:BS] + top[BS:] + dot(a[:BS], jnp.concatenate(xs_low, axis=0))


def each(n, body):
    def step(k, carry):
        body(k)
        return carry
    lax.fori_loop(0, n, step, 0)


def remote(src, dst, send, recv, device):
    return pltpu.make_async_remote_copy(
        src_ref=src, dst_ref=dst, send_sem=send, recv_sem=recv,
        device_id=device, device_id_type=MESH,
    )


def both(*conds):
    out = conds[0]
    for cond in conds[1:]:
        out = jnp.logical_and(out, cond)
    return out


def either(*conds):
    out = conds[0]
    for cond in conds[1:]:
        out = jnp.logical_or(out, cond)
    return out


def kernel(
    rows, cols,
    band1, band2, s_ref, a1_ref, a2_ref, out_ref,
    hb, hbh, hbl, a1f, a1s, a2f, a2s, stage, g0, g1, gh, gl, res, resin, band_mine, band_all, bands,
    own_send, direct_recv, far_send, far_recv,
    slab_send, slab_recv, chain_send, wide_send, wide_recv,
    band_send, band_recv, in_send, in_recv, share_send, share_recv, side_send, side_recv,
    back_send, back_recv, local_sem,
):
    r = lax.axis_index("row")
    c = lax.axis_index("col")
    y = c // 8
    q = c % 8
    h = q // 2
    core = q % 2
    owner = h // 2
    mine = q % 4
    base = 8 * y + 4 * core
    local_owner = core == owner
    x = r // 2
    p = r % 2
    mate = r + 1 - 2 * p
    other = c + 1 - 2 * core
    far_to = r + 2 - 4 * p
    far_from = r - 2 + 4 * p
    has_far_to = both(far_to >= 0, far_to < rows)
    has_far_from = both(far_from >= 0, far_from < rows)
    side = c - 7 + 14 * core
    has_side = both(side >= 0, side < cols)
    out_row = r + 1 - 2 * p
    out_h = (h + 3 + 2 * p) % 4

    load_own = pltpu.make_async_copy(s_ref, hb.at[pl.ds(8, 8)], local_sem.at[0])
    load_a1 = pltpu.make_async_copy(a1_ref, a1f, local_sem.at[1])
    load_a2 = pltpu.make_async_copy(a2_ref, a2f.at[mine], local_sem.at[2])
    load_own.start()
    load_a1.start()

    @pl.when(local_owner)
    def _():
        load_a2.start()

    barrier = pltpu.get_barrier_semaphore()

    def greet(device):
        pl.semaphore_signal(barrier, inc=1, device_id=device, device_id_type=MESH)

    for o in range(1, 8):
        greet((r, 8 * y + (q + o) % 8))
    for o in range(1, rows // 2):
        greet(((r + 2 * o) % rows, c))
    for k in range(2):
        greet((mate, 8 * y + 2 * h + k))
        greet((out_row, 8 * y + 2 * out_h + k))

    @pl.when(has_side)
    def _():
        greet((r, side))

    pl.semaphore_wait(barrier, 7 + rows // 2 - 1 + 4 + has_side.astype(jnp.int32))

    near_at = 16 - 16 * p
    away_at = 16 * p

    def send_own(k):
        return remote(s_ref.at[k], hb.at[16 * p + k], own_send.at[k], direct_recv.at[k], (mate, c))

    def got_direct(k):
        return remote(s_ref.at[k], hb.at[near_at + k], own_send.at[k], direct_recv.at[k], (mate, c))

    def send_far(k):
        return remote(hb.at[near_at + k], hb.at[16 * p + k], far_send.at[k], far_recv.at[k], (far_to, c))

    def got_far(k):
        return remote(hb.at[near_at + k], hb.at[away_at + k], far_send.at[k], far_recv.at[k], (mate, c))

    each(8, lambda k: send_own(k).start())

    part = BS // (rows // 2)

    def piece(m, at):
        return a2f.at[m, :, :, pl.ds(pl.multiple_of(part * at, part), part), :]

    slab_to_mate_core = remote(a2_ref, a2f.at[mine], slab_send.at[0], slab_recv.at[mine], (r, other))
    slab_out = remote(
        a2_ref.at[:, :, pl.ds(pl.multiple_of(part * x, part), part), :], piece(mine, x),
        slab_send.at[1], slab_recv.at[mine], (out_row, 8 * y + 2 * out_h + owner),
    )
    slab_out.start()

    @pl.when(jnp.logical_not(local_owner))
    def _():
        slab_to_mate_core.start()

    def far_of(m):
        return (2 * core + m // 2 - h + 4) % 4

    def chain_conds(m):
        d = far_of(m)
        from_origin = either(both(d == 3, p == 0), both(d == 1, p == 1))
        from_mate = either(both(d == 3, p == 1), both(d == 1, p == 0))
        return d, from_origin, from_mate

    def chain_copy(m, way):
        device = (mate, c) if way == 0 else (out_row, 8 * y + 2 * out_h + core)
        return remote(piece(m, x), piece(m, x), chain_send.at[m], slab_recv.at[m], device)

    def wide_copy(m, o):
        return remote(piece(m, x), piece(m, x), wide_send.at[m, o - 1], wide_recv.at[m, o - 1], ((r + 2 * o) % rows, c))

    def got_wide(m, o):
        at = (x - o + rows // 2) % (rows // 2)
        return remote(piece(m, x), piece(m, at), wide_send.at[m, o - 1], wide_recv.at[m, o - 1], (mate, c))

    def widen(m):
        for o in range(1, rows // 2):
            wide_copy(m, o).start()

    def origin_step(m):
        @pl.when(chain_conds(m)[1])
        def _():
            chain_copy(m, 0).wait_recv()
            chain_copy(m, 0).start()

    def origin_widen(m):
        @pl.when(chain_conds(m)[1])
        def _():
            widen(m)

    def mate_step(m):
        @pl.when(chain_conds(m)[2])
        def _():
            chain_copy(m, 1).wait_recv()
            chain_copy(m, 1).start()
            widen(m)

    def far_step(m):
        @pl.when(far_of(m) == 2)
        def _():
            chain_copy(m, 0).wait_recv()
            widen(m)

    row_id = lax.broadcasted_iota(jnp.int32, (8, BS), 0)
    lane_id = lax.broadcasted_iota(jnp.int32, (8, BS), 1)
    table = jnp.zeros((8, BS), jnp.int32)
    for j in range(2):
        for t in range(BAND):
            table = jnp.where(both(row_id == j, lane_id == t), band2[j, t], table)
    band_mine[...] = table

    @pl.when(local_owner)
    def _():
        band_all[mine] = table

    def group_copy(src, dst, send, recv, o):
        return remote(src, dst, send, recv, (r, 8 * y + 2 * ((h + o) % 4) + owner))

    def band_copy(o):
        return group_copy(band_mine, band_all.at[mine], band_send.at[o], band_recv.at[mine], o)

    def got_band(m):
        return remote(band_mine, band_all.at[m], band_send.at[0], band_recv.at[m], (mate, c))

    def is_remote(o):
        return jnp.logical_or(o != 0, jnp.logical_not(local_owner))

    for o in range(4):
        @pl.when(is_remote(o))
        def _():
            band_copy(o).start()

    load_own.wait()
    load_a1.wait()

    def split_rows(at):
        high, low = halves(hb[at])
        hbh[at] = high
        hbl[at] = low

    def halo_step(k):
        for t in range(BAND):
            high, low = halves(a1f[k, t])
            a1s[k, 0:BS, t * BS:(t + 1) * BS] = high
            a1s[k, BS:2 * BS, t * BS:(t + 1) * BS] = low
        split_rows(8 + k)
        got_direct(k).wait_recv()

        @pl.when(has_far_to)
        def _():
            send_far(k).start()

        split_rows(near_at + k)

    each(4, halo_step)
    each(4, origin_step)
    each(4, lambda k: halo_step(4 + k))
    each(4, origin_widen)

    @pl.when(has_far_from)
    def _():
        def step(k):
            got_far(k).wait_recv()
            split_rows(away_at + k)
        each(8, step)

    gs = (g0, g1)

    def in_copy(e, o):
        hp = (h + o) % 4
        return group_copy(stage.at[e, hp], gs[e].at[pl.ds(8 + 2 * mine, 2)], in_send.at[e, o], in_recv.at[e, mine], o)

    def got_in(e, m):
        return remote(stage.at[e, 0], gs[e].at[pl.ds(8 + 2 * m, 2)], in_send.at[e, 0], in_recv.at[e, m], (mate, c))

    for e in range(2):
        def advect(n, e=e):
            o = 3 - n
            hp = (h + o) % 4
            i = 2 * hp + e
            ids = [jnp.clip(band1[i, t] - 8 * r + REACH, 0, 23) for t in range(BAND)]
            tile = product(a1s[i], [hbh[k] for k in ids], [hbl[k] for k in ids])
            for b in range(2):
                stage[e, hp, b] = tile[:, b * BS:(b + 1) * BS].T

            @pl.when(is_remote(o))
            def _():
                in_copy(e, o).start()

            @pl.when(jnp.logical_not(is_remote(o)))
            def _():
                for b in range(2):
                    gs[e][8 + 2 * mine + b] = stage[e, hp, b]
        each(4, advect)
        if e == 0:
            each(4, mate_step)

    for m in range(4):
        @pl.when(base + m != c)
        def _():
            got_band(m).wait_recv()
    to_scalars = pltpu.make_async_copy(band_all, bands, local_sem.at[3])
    to_scalars.start()

    def share_copy(e, m):
        return remote(
            gs[e].at[pl.ds(8 + 2 * m, 2)], gs[e].at[pl.ds(16 * core + 2 * m, 2)],
            share_send.at[e, m], share_recv.at[e, m], (r, other),
        )

    def side_copy(e, m):
        return remote(
            gs[e].at[pl.ds(8 + 2 * m, 2)], gs[e].at[pl.ds(16 - 16 * core + 2 * m, 2)],
            side_send.at[e, m], side_recv.at[e, m], (r, side),
        )

    def got_share(e, m):
        return remote(
            gs[e].at[pl.ds(8 + 2 * m, 2)], gs[e].at[pl.ds(16 - 16 * core + 2 * m, 2)],
            share_send.at[e, m], share_recv.at[e, m], (r, other),
        )

    def got_side(e, m):
        return remote(
            gs[e].at[pl.ds(8 + 2 * m, 2)], gs[e].at[pl.ds(16 * core + 2 * m, 2)],
            side_send.at[e, m], side_recv.at[e, m], (r, other),
        )

    def back_copy(e, m):
        return remote(res.at[e, m], resin.at[e, h], back_send.at[e, m], back_recv.at[e, h], (r, base + m))

    def got_back(e, hp):
        return remote(res.at[e, 0], resin.at[e, hp], back_send.at[e, 0], back_recv.at[e, hp], (mate, c))

    def split_pair(e, at):
        for b in range(2):
            high, low = halves(gs[e][at + b])
            gh[e, at + b] = high
            gl[e, at + b] = low

    near = jnp.where(local_owner, h % 2, 1 - h % 2)

    def slab_step(m):
        @pl.when(both(far_of(m) == 0, base + m != c))
        def _():
            remote(a2_ref, a2f.at[m], slab_send.at[0], slab_recv.at[m], (r, other)).wait_recv()

        @pl.when(far_of(m) != 0)
        def _():
            for o in range(1, rows // 2):
                got_wide(m, o).wait_recv()

        for jj in range(2):
            for t in range(BAND):
                high, low = halves(a2f[m, jj, t])
                a2s[2 * m + jj, 0:BS, t * BS:(t + 1) * BS] = high
                a2s[2 * m + jj, BS:2 * BS, t * BS:(t + 1) * BS] = low

    def own_step(e, m):
        @pl.when(base + m != c)
        def _():
            got_in(e, m).wait_recv()

        share_copy(e, m).start()

        @pl.when(has_side)
        def _():
            side_copy(e, m).start()

        split_pair(e, 8 + 2 * m)

    def neighbour_step(e, m):
        got_share(e, m).wait_recv()
        split_pair(e, 16 - 16 * core + 2 * m)

        @pl.when(has_side)
        def _():
            got_side(e, m).wait_recv()
            split_pair(e, 16 * core + 2 * m)

    def second(e, m):
        for jj in range(2):
            ids = [jnp.clip(bands[m, jj, t] - 2 * base + REACH, 0, 23) for t in range(BAND)]
            res[e, m, jj] = product(a2s[2 * m + jj], [gh[e, k] for k in ids], [gl[e, k] for k in ids])

        @pl.when(base + m != c)
        def _():
            back_copy(e, m).start()

    each(4, lambda m: own_step(0, m))
    each(4, far_step)
    to_scalars.wait()

    @pl.when(local_owner)
    def _():
        load_a2.wait()

    each(2, lambda b: slab_step(2 * near + b))
    each(4, lambda m: neighbour_step(0, m))
    each(2, lambda b: second(0, 2 * near + b))
    each(4, lambda m: own_step(1, m))
    each(4, lambda m: neighbour_step(1, m))
    each(2, lambda b: second(1, 2 * near + b))
    each(2, lambda b: slab_step(2 - 2 * near + b))
    each(2, lambda b: second(0, 2 - 2 * near + b))
    each(2, lambda b: second(1, 2 - 2 * near + b))

    for e in range(2):
        def finish(hp, e=e):
            columns = pl.ds(pl.multiple_of((2 * hp + e) * BS, BS), BS)
            here = both(hp == h, local_owner)

            @pl.when(jnp.logical_not(here))
            def _():
                got_back(e, hp).wait_recv()
                for jj in range(2):
                    out_ref[jj * BS:(jj + 1) * BS, columns] = resin[e, hp, jj]

            @pl.when(here)
            def _():
                for jj in range(2):
                    out_ref[jj * BS:(jj + 1) * BS, columns] = res[e, mine, jj]

        each(4, finish)

    slab_out.wait_send()

    @pl.when(jnp.logical_not(local_owner))
    def _():
        slab_to_mate_core.wait_send()

    def drain_halo(k):
        send_own(k).wait_send()

        @pl.when(has_far_to)
        def _():
            send_far(k).wait_send()

    each(8, drain_halo)

    def drain(m):
        d, from_origin, from_mate = chain_conds(m)

        @pl.when(from_origin)
        def _():
            chain_copy(m, 0).wait_send()

        @pl.when(from_mate)
        def _():
            chain_copy(m, 1).wait_send()

        @pl.when(d != 0)
        def _():
            for o in range(1, rows // 2):
                wide_copy(m, o).wait_send()

        @pl.when(is_remote(m))
        def _():
            band_copy(m).wait_send()
            for e in range(2):
                in_copy(e, m).wait_send()

        for e in range(2):
            share_copy(e, m).wait_send()

            @pl.when(has_side)
            def _():
                side_copy(e, m).wait_send()

            @pl.when(base + m != c)
            def _():
                back_copy(e, m).wait_send()

    each(4, drain)


def solution(mesh):
    rows, cols = mesh.shape["row"], mesh.shape["col"]

    def body(state_cov, trans_first, band_first, trans_second, band_second, noise_cov):
        width = state_cov.shape[1]
        tiles = state_cov.reshape(8, BS, width)
        f32, bf16, i32 = jnp.float32, jnp.bfloat16, jnp.int32
        smem = pl.BlockSpec(memory_space=pltpu.SMEM)
        anyspace = pl.BlockSpec(memory_space=pl.ANY)
        dma = pltpu.SemaphoreType.DMA
        product_t = pl.pallas_call(
            lambda *refs: kernel(rows, cols, *refs),
            out_shape=jax.ShapeDtypeStruct((width, 8 * BS), f32),
            in_specs=[smem, smem, anyspace, anyspace, anyspace],
            out_specs=pl.BlockSpec(memory_space=pltpu.VMEM),
            scratch_shapes=[
                pltpu.VMEM((24, BS, width), f32),
                pltpu.VMEM((24, BS, width), bf16),
                pltpu.VMEM((24, BS, width), bf16),
                pltpu.VMEM((8, BAND, BS, BS), f32),
                pltpu.VMEM((8, 2 * BS, BAND * BS), bf16),
                pltpu.VMEM((4, 2, BAND, BS, BS), f32),
                pltpu.VMEM((8, 2 * BS, BAND * BS), bf16),
                pltpu.VMEM((2, 4, 2, BS, BS), f32),
                pltpu.VMEM((24, BS, BS), f32),
                pltpu.VMEM((24, BS, BS), f32),
                pltpu.VMEM((2, 24, BS, BS), bf16),
                pltpu.VMEM((2, 24, BS, BS), bf16),
                pltpu.VMEM((2, 4, 2, BS, BS), f32),
                pltpu.VMEM((2, 4, 2, BS, BS), f32),
                pltpu.VMEM((8, BS), i32),
                pltpu.VMEM((4, 8, BS), i32),
                pltpu.SMEM((4, 8, BS), i32),
                dma((8,)), dma((8,)), dma((8,)), dma((8,)),
                dma((2,)), dma((4,)), dma((4,)), dma((4, 3)), dma((4, 3)),
                dma((4,)), dma((4,)), dma((2, 4)), dma((2, 4)),
                dma((2, 4)), dma((2, 4)), dma((2, 4)), dma((2, 4)),
                dma((2, 4)), dma((2, 4)), dma((4,)),
            ],
            compiler_params=pltpu.CompilerParams(
                collective_id=0, has_side_effects=True, vmem_limit_bytes=60 * 2**20
            ),
            name="forecast",
        )(band_first, band_second, tiles, trans_first, trans_second)
        return product_t + noise_cov

    return jax.shard_map(
        body,
        mesh=mesh,
        in_specs=(
            P("row", "col"),
            P("row", None, None, None),
            P("row", None),
            P("col", None, None, None),
            P("col", None),
            P("col", "row"),
        ),
        out_specs=P("col", "row"),
        check_vma=False,
    )
```

```python
import jax
import jax.numpy as jnp
from jax import lax
from jax.experimental import pallas as pl
from jax.experimental.pallas import tpu as pltpu
from jax.sharding import PartitionSpec as P

BAND = 9
REACH = 8
BS = 128
MESH = pl.DeviceIdType.MESH


def halves(x):
    high = x.astype(jnp.bfloat16)
    low = (x - high.astype(jnp.float32)).astype(jnp.bfloat16)
    return high, low


def dot(a, b):
    return jnp.dot(a, b, preferred_element_type=jnp.float32)


def product(a, xs_high, xs_low):
    top = dot(a, jnp.concatenate(xs_high, axis=0))
    return top[:BS] + top[BS:] + dot(a[:BS], jnp.concatenate(xs_low, axis=0))


def each(n, body):
    def step(k, carry):
        body(k)
        return carry
    lax.fori_loop(0, n, step, 0)


def remote(src, dst, send, recv, device):
    return pltpu.make_async_remote_copy(
        src_ref=src, dst_ref=dst, send_sem=send, recv_sem=recv,
        device_id=device, device_id_type=MESH,
    )


def both(*conds):
    out = conds[0]
    for cond in conds[1:]:
        out = jnp.logical_and(out, cond)
    return out


def either(*conds):
    out = conds[0]
    for cond in conds[1:]:
        out = jnp.logical_or(out, cond)
    return out


def kernel(
    rows, cols,
    band1, band2, s_ref, a1_ref, a2_ref, out_ref,
    hb, hbh, hbl, a1f, a1s, a2f, a2s, stage, g0, g1, gh, gl, res, resin, band_mine, band_all, bands,
    own_send, direct_recv, far_send, far_recv,
    slab_send, slab_recv, chain_send, wide_send, wide_recv,
    band_send, band_recv, in_send, in_recv, share_send, share_recv, side_send, side_recv,
    back_send, back_recv, local_sem,
):
    r = lax.axis_index("row")
    c = lax.axis_index("col")
    y = c // 8
    q = c % 8
    h = q // 2
    core = q % 2
    owner = h // 2
    mine = q % 4
    base = 8 * y + 4 * core
    local_owner = core == owner
    x = r // 2
    p = r % 2
    mate = r + 1 - 2 * p
    other = c + 1 - 2 * core
    far_to = r + 2 - 4 * p
    far_from = r - 2 + 4 * p
    has_far_to = both(far_to >= 0, far_to < rows)
    has_far_from = both(far_from >= 0, far_from < rows)
    side = c - 7 + 14 * core
    has_side = both(side >= 0, side < cols)
    out_row = r + 1 - 2 * p
    out_h = (h + 3 + 2 * p) % 4

    def half(b):
        return slice(b * BS, (b + 1) * BS)

    loads_own = [
        pltpu.make_async_copy(s_ref.at[:, :, half(b)], hb.at[b, pl.ds(8, 8)], local_sem.at[b]) for b in range(2)
    ]
    load_a1 = pltpu.make_async_copy(a1_ref, a1f, local_sem.at[2])
    load_a2 = pltpu.make_async_copy(a2_ref, a2f.at[mine], local_sem.at[3])
    loads_own[0].start()
    load_a1.start()
    loads_own[1].start()

    @pl.when(local_owner)
    def _():
        load_a2.start()

    barrier = pltpu.get_barrier_semaphore()

    def greet(device):
        pl.semaphore_signal(barrier, inc=1, device_id=device, device_id_type=MESH)

    for o in range(1, 8):
        greet((r, 8 * y + (q + o) % 8))
    for o in range(1, rows // 2):
        greet(((r + 2 * o) % rows, c))
    for k in range(2):
        greet((mate, 8 * y + 2 * h + k))
        greet((out_row, 8 * y + 2 * out_h + k))

    @pl.when(has_side)
    def _():
        greet((r, side))

    pl.semaphore_wait(barrier, 7 + rows // 2 - 1 + 4 + has_side.astype(jnp.int32))

    near_at = 16 - 16 * p
    away_at = 16 * p

    def send_own(b, k):
        return remote(
            s_ref.at[pl.ds(2 * k, 2), :, half(b)], hb.at[b, pl.ds(16 * p + 2 * k, 2)],
            own_send.at[b, k], direct_recv.at[b, k], (mate, c),
        )

    def send_far(b, k):
        return remote(
            hb.at[b, pl.ds(near_at + 2 * k, 2)], hb.at[b, pl.ds(16 * p + 2 * k, 2)],
            far_send.at[b, k], far_recv.at[b, k], (far_to, c),
        )

    def got_direct(b, k):
        at = hb.at[b, pl.ds(near_at + 2 * k, 2)]
        return remote(at, at, own_send.at[b, k], direct_recv.at[b, k], (mate, c))

    def got_far(b, k):
        at = hb.at[b, pl.ds(away_at + 2 * k, 2)]
        return remote(at, at, far_send.at[b, k], far_recv.at[b, k], (mate, c))

    each(4, lambda k: send_own(0, k).start())

    part = BS // (rows // 2)

    def piece(m, at):
        return a2f.at[m, :, :, pl.ds(pl.multiple_of(part * at, part), part), :]

    slab_to_mate_core = remote(a2_ref, a2f.at[mine], slab_send.at[0], slab_recv.at[mine], (r, other))
    slab_out = remote(
        a2_ref.at[:, :, pl.ds(pl.multiple_of(part * x, part), part), :], piece(mine, x),
        slab_send.at[1], slab_recv.at[mine], (out_row, 8 * y + 2 * out_h + owner),
    )
    slab_out.start()

    @pl.when(jnp.logical_not(local_owner))
    def _():
        slab_to_mate_core.start()

    def far_of(m):
        return (2 * core + m // 2 - h + 4) % 4

    def chain_conds(m):
        d = far_of(m)
        from_origin = either(both(d == 3, p == 0), both(d == 1, p == 1))
        from_mate = either(both(d == 3, p == 1), both(d == 1, p == 0))
        return d, from_origin, from_mate

    def chain_copy(m, way):
        device = (mate, c) if way == 0 else (out_row, 8 * y + 2 * out_h + core)
        return remote(piece(m, x), piece(m, x), chain_send.at[m], slab_recv.at[m], device)

    def wide_copy(m, o):
        return remote(piece(m, x), piece(m, x), wide_send.at[m, o - 1], wide_recv.at[m, o - 1], ((r + 2 * o) % rows, c))

    def got_wide(m, o):
        at = (x - o + rows // 2) % (rows // 2)
        return remote(piece(m, x), piece(m, at), wide_send.at[m, o - 1], wide_recv.at[m, o - 1], (mate, c))

    def widen(m):
        for o in range(1, rows // 2):
            wide_copy(m, o).start()

    def origin_step(m):
        @pl.when(chain_conds(m)[1])
        def _():
            chain_copy(m, 0).wait_recv()
            chain_copy(m, 0).start()

    def origin_widen(m):
        @pl.when(chain_conds(m)[1])
        def _():
            widen(m)

    def mate_step(m):
        @pl.when(chain_conds(m)[2])
        def _():
            chain_copy(m, 1).wait_recv()
            chain_copy(m, 1).start()

    def mate_widen(m):
        @pl.when(chain_conds(m)[2])
        def _():
            widen(m)

    def far_step(m):
        @pl.when(far_of(m) == 2)
        def _():
            chain_copy(m, 0).wait_recv()
            widen(m)

    row_id = lax.broadcasted_iota(jnp.int32, (8, BS), 0)
    lane_id = lax.broadcasted_iota(jnp.int32, (8, BS), 1)
    table = jnp.zeros((8, BS), jnp.int32)
    for j in range(2):
        for t in range(BAND):
            table = jnp.where(both(row_id == j, lane_id == t), band2[j, t], table)
    band_mine[...] = table

    @pl.when(local_owner)
    def _():
        band_all[mine] = table

    def group_copy(src, dst, send, recv, o):
        return remote(src, dst, send, recv, (r, 8 * y + 2 * ((h + o) % 4) + owner))

    def band_copy(o):
        return group_copy(band_mine, band_all.at[mine], band_send.at[o], band_recv.at[mine], o)

    def got_band(m):
        return remote(band_mine, band_all.at[m], band_send.at[0], band_recv.at[m], (mate, c))

    def is_remote(o):
        return jnp.logical_or(o != 0, jnp.logical_not(local_owner))

    for o in range(4):
        @pl.when(is_remote(o))
        def _():
            band_copy(o).start()

    loads_own[0].wait()
    load_a1.wait()

    def split_rows(b, at):
        for n in range(2):
            high, low = halves(hb[b, at + n])
            hbh[b, at + n] = high
            hbl[b, at + n] = low

    def split_first(i):
        for t in range(BAND):
            high, low = halves(a1f[i, t])
            a1s[i, 0:BS, t * BS:(t + 1) * BS] = high
            a1s[i, BS:2 * BS, t * BS:(t + 1) * BS] = low

    def direct_step(b, k):
        split_rows(b, 8 + 2 * k)
        got_direct(b, k).wait_recv()

        @pl.when(has_far_to)
        def _():
            send_far(b, k).start()

        split_rows(b, near_at + 2 * k)

    def away_step(b, k):
        @pl.when(has_far_from)
        def _():
            got_far(b, k).wait_recv()
            split_rows(b, away_at + 2 * k)

    gs = (g0, g1)

    def in_copy(b, e, o):
        hp = (h + o) % 4
        return group_copy(
            stage.at[e, hp, b], gs[e].at[8 + 2 * mine + b], in_send.at[b, e, o], in_recv.at[b, e, mine], o
        )

    def got_in(b, e, m):
        at = gs[e].at[8 + 2 * m + b]
        return remote(at, at, in_send.at[b, e, 0], in_recv.at[b, e, m], (mate, c))

    def advect(b, e, n):
        o = 3 - n
        hp = (h + o) % 4
        i = 2 * hp + e
        ids = [jnp.clip(band1[i, t] - 8 * r + REACH, 0, 23) for t in range(BAND)]
        tile = product(a1s[i], [hbh[b, k] for k in ids], [hbl[b, k] for k in ids]).T
        stage[e, hp, b] = tile

        @pl.when(is_remote(o))
        def _():
            in_copy(b, e, o).start()

        @pl.when(jnp.logical_not(is_remote(o)))
        def _():
            gs[e][8 + 2 * mine + b] = tile

    def first_step(k):
        for n in range(2):
            split_first(2 * k + n)
        direct_step(0, k)

    each(3, first_step)
    each(4, origin_step)
    each(4, lambda k: send_own(1, k).start())
    first_step(3)
    each(4, origin_widen)
    loads_own[1].wait()
    each(4, lambda k: away_step(0, k))
    each(4, lambda n: advect(0, 0, n))
    each(4, mate_step)
    each(4, lambda n: advect(0, 1, n))
    each(4, lambda k: direct_step(1, k))
    each(4, mate_widen)
    each(4, lambda k: away_step(1, k))
    each(4, lambda n: advect(1, 0, n))
    each(4, lambda n: advect(1, 1, n))

    for m in range(4):
        @pl.when(base + m != c)
        def _():
            got_band(m).wait_recv()
    to_scalars = pltpu.make_async_copy(band_all, bands, local_sem.at[4])
    to_scalars.start()

    def share_copy(b, e, m):
        return remote(
            gs[e].at[8 + 2 * m + b], gs[e].at[16 * core + 2 * m + b],
            share_send.at[b, e, m], share_recv.at[b, e, m], (r, other),
        )

    def side_copy(b, e, m):
        return remote(
            gs[e].at[8 + 2 * m + b], gs[e].at[16 - 16 * core + 2 * m + b],
            side_send.at[b, e, m], side_recv.at[b, e, m], (r, side),
        )

    def got_share(b, e, m):
        at = gs[e].at[16 - 16 * core + 2 * m + b]
        return remote(at, at, share_send.at[b, e, m], share_recv.at[b, e, m], (r, other))

    def got_side(b, e, m):
        at = gs[e].at[16 * core + 2 * m + b]
        return remote(at, at, side_send.at[b, e, m], side_recv.at[b, e, m], (r, other))

    def back_copy(e, m):
        return remote(res.at[e, m], resin.at[e, h], back_send.at[e, m], back_recv.at[e, h], (r, base + m))

    def got_back(e, hp):
        return remote(res.at[e, 0], resin.at[e, hp], back_send.at[e, 0], back_recv.at[e, hp], (mate, c))

    def split_block(e, at):
        high, low = halves(gs[e][at])
        gh[e, at] = high
        gl[e, at] = low

    near = jnp.where(local_owner, h % 2, 1 - h % 2)

    def slab_step(m):
        @pl.when(both(far_of(m) == 0, base + m != c))
        def _():
            remote(a2_ref, a2f.at[m], slab_send.at[0], slab_recv.at[m], (r, other)).wait_recv()

        @pl.when(far_of(m) != 0)
        def _():
            for o in range(1, rows // 2):
                got_wide(m, o).wait_recv()

        for jj in range(2):
            for t in range(BAND):
                high, low = halves(a2f[m, jj, t])
                a2s[2 * m + jj, 0:BS, t * BS:(t + 1) * BS] = high
                a2s[2 * m + jj, BS:2 * BS, t * BS:(t + 1) * BS] = low

    def own_step(b, e, m):
        @pl.when(base + m != c)
        def _():
            got_in(b, e, m).wait_recv()

        share_copy(b, e, m).start()

        @pl.when(has_side)
        def _():
            side_copy(b, e, m).start()

        split_block(e, 8 + 2 * m + b)

    def neighbour_step(b, e, m):
        got_share(b, e, m).wait_recv()
        split_block(e, 16 - 16 * core + 2 * m + b)

        @pl.when(has_side)
        def _():
            got_side(b, e, m).wait_recv()
            split_block(e, 16 * core + 2 * m + b)

    def second(e, m):
        for jj in range(2):
            ids = [jnp.clip(bands[m, jj, t] - 2 * base + REACH, 0, 23) for t in range(BAND)]
            res[e, m, jj] = product(a2s[2 * m + jj], [gh[e, k] for k in ids], [gl[e, k] for k in ids])

        @pl.when(base + m != c)
        def _():
            back_copy(e, m).start()

    for e in range(2):
        each(4, lambda m: own_step(0, e, m))
    each(4, far_step)
    to_scalars.wait()

    @pl.when(local_owner)
    def _():
        load_a2.wait()

    for e in range(2):
        each(4, lambda m: own_step(1, e, m))
        if e == 0:
            each(2, lambda n: slab_step(2 * near + n))
        for b in range(2):
            each(4, lambda m: neighbour_step(b, e, m))
        each(2, lambda n: second(e, 2 * near + n))
        if e == 0:
            each(2, lambda n: slab_step(2 - 2 * near + n))
        each(2, lambda n: second(e, 2 - 2 * near + n))

    for e in range(2):
        def finish(hp, e=e):
            columns = pl.ds(pl.multiple_of((2 * hp + e) * BS, BS), BS)
            here = both(hp == h, local_owner)

            @pl.when(jnp.logical_not(here))
            def _():
                got_back(e, hp).wait_recv()
                for jj in range(2):
                    out_ref[jj * BS:(jj + 1) * BS, columns] = resin[e, hp, jj]

            @pl.when(here)
            def _():
                for jj in range(2):
                    out_ref[jj * BS:(jj + 1) * BS, columns] = res[e, mine, jj]

        each(4, finish)

    slab_out.wait_send()

    @pl.when(jnp.logical_not(local_owner))
    def _():
        slab_to_mate_core.wait_send()

    def drain_halo(k):
        for b in range(2):
            send_own(b, k).wait_send()

            @pl.when(has_far_to)
            def _():
                send_far(b, k).wait_send()

    each(4, drain_halo)

    def drain(m):
        d, from_origin, from_mate = chain_conds(m)

        @pl.when(from_origin)
        def _():
            chain_copy(m, 0).wait_send()

        @pl.when(from_mate)
        def _():
            chain_copy(m, 1).wait_send()

        @pl.when(d != 0)
        def _():
            for o in range(1, rows // 2):
                wide_copy(m, o).wait_send()

        @pl.when(is_remote(m))
        def _():
            band_copy(m).wait_send()
            for e in range(2):
                for b in range(2):
                    in_copy(b, e, m).wait_send()

        for e in range(2):
            for b in range(2):
                share_copy(b, e, m).wait_send()

                @pl.when(has_side)
                def _():
                    side_copy(b, e, m).wait_send()

            @pl.when(base + m != c)
            def _():
                back_copy(e, m).wait_send()

    each(4, drain)


def solution(mesh):
    rows, cols = mesh.shape["row"], mesh.shape["col"]

    def body(state_cov, trans_first, band_first, trans_second, band_second, noise_cov):
        width = state_cov.shape[1]
        tiles = state_cov.reshape(8, BS, width)
        f32, bf16, i32 = jnp.float32, jnp.bfloat16, jnp.int32
        smem = pl.BlockSpec(memory_space=pltpu.SMEM)
        anyspace = pl.BlockSpec(memory_space=pl.ANY)
        dma = pltpu.SemaphoreType.DMA
        product_t = pl.pallas_call(
            lambda *refs: kernel(rows, cols, *refs),
            out_shape=jax.ShapeDtypeStruct((width, 8 * BS), f32),
            in_specs=[smem, smem, anyspace, anyspace, anyspace],
            out_specs=pl.BlockSpec(memory_space=pltpu.VMEM),
            scratch_shapes=[
                pltpu.VMEM((2, 24, BS, BS), f32),
                pltpu.VMEM((2, 24, BS, BS), bf16),
                pltpu.VMEM((2, 24, BS, BS), bf16),
                pltpu.VMEM((8, BAND, BS, BS), f32),
                pltpu.VMEM((8, 2 * BS, BAND * BS), bf16),
                pltpu.VMEM((4, 2, BAND, BS, BS), f32),
                pltpu.VMEM((8, 2 * BS, BAND * BS), bf16),
                pltpu.VMEM((2, 4, 2, BS, BS), f32),
                pltpu.VMEM((24, BS, BS), f32),
                pltpu.VMEM((24, BS, BS), f32),
                pltpu.VMEM((2, 24, BS, BS), bf16),
                pltpu.VMEM((2, 24, BS, BS), bf16),
                pltpu.VMEM((2, 4, 2, BS, BS), f32),
                pltpu.VMEM((2, 4, 2, BS, BS), f32),
                pltpu.VMEM((8, BS), i32),
                pltpu.VMEM((4, 8, BS), i32),
                pltpu.SMEM((4, 8, BS), i32),
                dma((2, 4)), dma((2, 4)), dma((2, 4)), dma((2, 4)),
                dma((2,)), dma((4,)), dma((4,)), dma((4, 3)), dma((4, 3)),
                dma((4,)), dma((4,)), dma((2, 2, 4)), dma((2, 2, 4)),
                dma((2, 2, 4)), dma((2, 2, 4)), dma((2, 2, 4)), dma((2, 2, 4)),
                dma((2, 4)), dma((2, 4)), dma((5,)),
            ],
            compiler_params=pltpu.CompilerParams(
                collective_id=0, has_side_effects=True, vmem_limit_bytes=52 * 2**20
            ),
            name="forecast",
        )(band_first, band_second, tiles, trans_first, trans_second)
        return product_t + noise_cov

    return jax.shard_map(
        body,
        mesh=mesh,
        in_specs=(
            P("row", "col"),
            P("row", None, None, None),
            P("row", None),
            P("col", None, None, None),
            P("col", None),
            P("col", "row"),
        ),
        out_specs=P("col", "row"),
        check_vma=False,
    )
```

```python
import jax
import jax.numpy as jnp
from jax import lax
from jax.experimental import pallas as pl
from jax.experimental.pallas import tpu as pltpu
from jax.sharding import PartitionSpec as P

BAND = 9
REACH = 8
BS = 128
MESH = pl.DeviceIdType.MESH


def halves(x):
    high = x.astype(jnp.bfloat16)
    low = (x - high.astype(jnp.float32)).astype(jnp.bfloat16)
    return high, low


def dot(a, b):
    return jnp.dot(a, b, preferred_element_type=jnp.float32)


def product(a, xs_high, xs_low):
    top = dot(a, jnp.concatenate(xs_high, axis=0))
    return top[:BS] + top[BS:] + dot(a[:BS], jnp.concatenate(xs_low, axis=0))


def each(n, body):
    def step(k, carry):
        body(k)
        return carry
    lax.fori_loop(0, n, step, 0)


def remote(src, dst, send, recv, device):
    return pltpu.make_async_remote_copy(
        src_ref=src, dst_ref=dst, send_sem=send, recv_sem=recv,
        device_id=device, device_id_type=MESH,
    )


def both(*conds):
    out = conds[0]
    for cond in conds[1:]:
        out = jnp.logical_and(out, cond)
    return out


def either(*conds):
    out = conds[0]
    for cond in conds[1:]:
        out = jnp.logical_or(out, cond)
    return out


def kernel(
    rows, cols,
    band1, band2, s_ref, a1_ref, a2_ref, out_ref,
    hb, hbh, hbl, a1f, a1s, a2f, a2s, stage, g0, g1, gh, gl, res, resin, band_mine, band_all, bands,
    own_send, direct_recv, far_send, far_recv,
    slab_send, slab_recv, chain_send, wide_send, wide_recv,
    band_send, band_recv, in_send, in_recv, share_send, share_recv, side_send, side_recv,
    back_send, back_recv, local_sem,
):
    r = lax.axis_index("row")
    c = lax.axis_index("col")
    y = c // 8
    q = c % 8
    h = q // 2
    core = q % 2
    owner = h // 2
    mine = q % 4
    base = 8 * y + 4 * core
    local_owner = core == owner
    x = r // 2
    p = r % 2
    mate = r + 1 - 2 * p
    other = c + 1 - 2 * core
    far_to = r + 2 - 4 * p
    far_from = r - 2 + 4 * p
    has_far_to = both(far_to >= 0, far_to < rows)
    has_far_from = both(far_from >= 0, far_from < rows)
    side = c - 7 + 14 * core
    has_side = both(side >= 0, side < cols)
    out_row = r + 1 - 2 * p
    out_h = (h + 3 + 2 * p) % 4

    def half(b):
        return slice(b * BS, (b + 1) * BS)

    loads_own = [
        pltpu.make_async_copy(s_ref.at[:, :, half(b)], hb.at[b, pl.ds(8, 8)], local_sem.at[b]) for b in range(2)
    ]
    load_a1 = pltpu.make_async_copy(a1_ref, a1f, local_sem.at[2])
    load_a2 = pltpu.make_async_copy(a2_ref, a2f.at[mine], local_sem.at[3])
    loads_own[0].start()
    load_a1.start()
    loads_own[1].start()

    @pl.when(local_owner)
    def _():
        load_a2.start()

    barrier = pltpu.get_barrier_semaphore()

    def greet(device):
        pl.semaphore_signal(barrier, inc=1, device_id=device, device_id_type=MESH)

    for o in range(1, 8):
        greet((r, 8 * y + (q + o) % 8))
    for o in range(1, rows // 2):
        greet(((r + 2 * o) % rows, c))
    for k in range(2):
        greet((mate, 8 * y + 2 * h + k))
        greet((out_row, 8 * y + 2 * out_h + k))

    @pl.when(has_side)
    def _():
        greet((r, side))

    pl.semaphore_wait(barrier, 7 + rows // 2 - 1 + 4 + has_side.astype(jnp.int32))

    near_at = 16 - 16 * p
    away_at = 16 * p

    def send_own(b, k):
        return remote(
            s_ref.at[pl.ds(2 * k, 2), :, half(b)], hb.at[b, pl.ds(16 * p + 2 * k, 2)],
            own_send.at[b, k], direct_recv.at[b, k], (mate, c),
        )

    def send_far(b, k):
        return remote(
            hb.at[b, pl.ds(near_at + 2 * k, 2)], hb.at[b, pl.ds(16 * p + 2 * k, 2)],
            far_send.at[b, k], far_recv.at[b, k], (far_to, c),
        )

    def got_direct(b, k):
        at = hb.at[b, pl.ds(near_at + 2 * k, 2)]
        return remote(at, at, own_send.at[b, k], direct_recv.at[b, k], (mate, c))

    def got_far(b, k):
        at = hb.at[b, pl.ds(away_at + 2 * k, 2)]
        return remote(at, at, far_send.at[b, k], far_recv.at[b, k], (mate, c))

    each(4, lambda k: send_own(0, k).start())

    part = BS // (rows // 2)

    def piece(m, at):
        return a2f.at[m, :, :, pl.ds(pl.multiple_of(part * at, part), part), :]

    slab_to_mate_core = remote(a2_ref, a2f.at[mine], slab_send.at[0], slab_recv.at[mine], (r, other))
    slab_out = remote(
        a2_ref.at[:, :, pl.ds(pl.multiple_of(part * x, part), part), :], piece(mine, x),
        slab_send.at[1], slab_recv.at[mine], (out_row, 8 * y + 2 * out_h + owner),
    )
    slab_out.start()

    @pl.when(jnp.logical_not(local_owner))
    def _():
        slab_to_mate_core.start()

    def far_of(m):
        return (2 * core + m // 2 - h + 4) % 4

    def chain_conds(m):
        d = far_of(m)
        from_origin = either(both(d == 3, p == 0), both(d == 1, p == 1))
        from_mate = either(both(d == 3, p == 1), both(d == 1, p == 0))
        return d, from_origin, from_mate

    def chain_copy(m, way):
        device = (mate, c) if way == 0 else (out_row, 8 * y + 2 * out_h + core)
        return remote(piece(m, x), piece(m, x), chain_send.at[m], slab_recv.at[m], device)

    def wide_copy(m, o):
        return remote(piece(m, x), piece(m, x), wide_send.at[m, o - 1], wide_recv.at[m, o - 1], ((r + 2 * o) % rows, c))

    def got_wide(m, o):
        at = (x - o + rows // 2) % (rows // 2)
        return remote(piece(m, x), piece(m, at), wide_send.at[m, o - 1], wide_recv.at[m, o - 1], (mate, c))

    def relay_copy(m):
        odd = m % 2
        at = (x + 3 - 2 * odd) % 4
        return remote(
            piece(m, at), piece(m, at), wide_send.at[m, 1], wide_recv.at[m, 1], ((r + 2 - 4 * odd + rows) % rows, c)
        )

    def widen(m):
        for o in (1, 3):
            wide_copy(m, o).start()

    def relay(m):
        got_wide(m, 1 + 2 * (m % 2)).wait_recv()
        relay_copy(m).start()

    def relay_step(m, kind):
        cond = far_of(m) == 2 if kind == 0 else chain_conds(m)[kind]

        @pl.when(cond)
        def _():
            relay(m)

    def origin_step(m):
        @pl.when(chain_conds(m)[1])
        def _():
            chain_copy(m, 0).wait_recv()
            chain_copy(m, 0).start()

    def origin_widen(m):
        @pl.when(chain_conds(m)[1])
        def _():
            widen(m)

    def mate_step(m):
        @pl.when(chain_conds(m)[2])
        def _():
            chain_copy(m, 1).wait_recv()
            chain_copy(m, 1).start()

    def mate_widen(m):
        @pl.when(chain_conds(m)[2])
        def _():
            widen(m)

    def far_step(m):
        @pl.when(far_of(m) == 2)
        def _():
            chain_copy(m, 0).wait_recv()
            widen(m)

    row_id = lax.broadcasted_iota(jnp.int32, (8, BS), 0)
    lane_id = lax.broadcasted_iota(jnp.int32, (8, BS), 1)
    table = jnp.zeros((8, BS), jnp.int32)
    for j in range(2):
        for t in range(BAND):
            table = jnp.where(both(row_id == j, lane_id == t), band2[j, t], table)
    band_mine[...] = table

    @pl.when(local_owner)
    def _():
        band_all[mine] = table

    def group_copy(src, dst, send, recv, o):
        return remote(src, dst, send, recv, (r, 8 * y + 2 * ((h + o) % 4) + owner))

    def band_copy(o):
        return group_copy(band_mine, band_all.at[mine], band_send.at[o], band_recv.at[mine], o)

    def got_band(m):
        return remote(band_mine, band_all.at[m], band_send.at[0], band_recv.at[m], (mate, c))

    def is_remote(o):
        return jnp.logical_or(o != 0, jnp.logical_not(local_owner))

    for o in range(4):
        @pl.when(is_remote(o))
        def _():
            band_copy(o).start()

    loads_own[0].wait()
    load_a1.wait()

    def split_rows(b, at):
        for n in range(2):
            high, low = halves(hb[b, at + n])
            hbh[b, at + n] = high
            hbl[b, at + n] = low

    def split_first(i):
        for t in range(BAND):
            high, low = halves(a1f[i, t])
            a1s[i, 0:BS, t * BS:(t + 1) * BS] = high
            a1s[i, BS:2 * BS, t * BS:(t + 1) * BS] = low

    def direct_step(b, k):
        split_rows(b, 8 + 2 * k)
        got_direct(b, k).wait_recv()

        @pl.when(has_far_to)
        def _():
            send_far(b, k).start()

        split_rows(b, near_at + 2 * k)

    def away_step(b, k):
        @pl.when(has_far_from)
        def _():
            got_far(b, k).wait_recv()
            split_rows(b, away_at + 2 * k)

    gs = (g0, g1)

    def in_copy(b, e, o):
        hp = (h + o) % 4
        return group_copy(
            stage.at[e, hp, b], gs[e].at[8 + 2 * mine + b], in_send.at[b, e, o], in_recv.at[b, e, mine], o
        )

    def got_in(b, e, m):
        at = gs[e].at[8 + 2 * m + b]
        return remote(at, at, in_send.at[b, e, 0], in_recv.at[b, e, m], (mate, c))

    def advect(b, e, n):
        o = 3 - n
        hp = (h + o) % 4
        i = 2 * hp + e
        ids = [jnp.clip(band1[i, t] - 8 * r + REACH, 0, 23) for t in range(BAND)]
        tile = product(a1s[i], [hbh[b, k] for k in ids], [hbl[b, k] for k in ids]).T
        stage[e, hp, b] = tile

        @pl.when(is_remote(o))
        def _():
            in_copy(b, e, o).start()

        @pl.when(jnp.logical_not(is_remote(o)))
        def _():
            gs[e][8 + 2 * mine + b] = tile

    def first_step(k):
        for n in range(2):
            split_first(2 * k + n)
        direct_step(0, k)

    each(3, first_step)
    each(4, origin_step)
    each(4, lambda k: send_own(1, k).start())
    first_step(3)
    each(4, origin_widen)
    loads_own[1].wait()
    each(4, lambda k: away_step(0, k))
    each(4, lambda n: advect(0, 0, n))
    each(4, mate_step)
    each(4, lambda n: advect(0, 1, n))
    each(4, lambda k: direct_step(1, k))
    each(4, lambda m: relay_step(m, 1))
    each(4, mate_widen)
    each(4, lambda k: away_step(1, k))
    each(4, lambda n: advect(1, 0, n))
    each(4, lambda n: advect(1, 1, n))

    for m in range(4):
        @pl.when(base + m != c)
        def _():
            got_band(m).wait_recv()
    to_scalars = pltpu.make_async_copy(band_all, bands, local_sem.at[4])
    to_scalars.start()

    def share_copy(b, e, m):
        return remote(
            gs[e].at[8 + 2 * m + b], gs[e].at[16 * core + 2 * m + b],
            share_send.at[b, e, m], share_recv.at[b, e, m], (r, other),
        )

    def side_copy(b, e, m):
        return remote(
            gs[e].at[8 + 2 * m + b], gs[e].at[16 - 16 * core + 2 * m + b],
            side_send.at[b, e, m], side_recv.at[b, e, m], (r, side),
        )

    def got_share(b, e, m):
        at = gs[e].at[16 - 16 * core + 2 * m + b]
        return remote(at, at, share_send.at[b, e, m], share_recv.at[b, e, m], (r, other))

    def got_side(b, e, m):
        at = gs[e].at[16 * core + 2 * m + b]
        return remote(at, at, side_send.at[b, e, m], side_recv.at[b, e, m], (r, other))

    def back_copy(e, m):
        return remote(res.at[e, m], resin.at[e, h], back_send.at[e, m], back_recv.at[e, h], (r, base + m))

    def got_back(e, hp):
        return remote(res.at[e, 0], resin.at[e, hp], back_send.at[e, 0], back_recv.at[e, hp], (mate, c))

    def split_block(e, at):
        high, low = halves(gs[e][at])
        gh[e, at] = high
        gl[e, at] = low

    near = jnp.where(local_owner, h % 2, 1 - h % 2)

    def slab_step(m):
        @pl.when(both(far_of(m) == 0, base + m != c))
        def _():
            remote(a2_ref, a2f.at[m], slab_send.at[0], slab_recv.at[m], (r, other)).wait_recv()

        @pl.when(far_of(m) != 0)
        def _():
            got_wide(m, 3 - 2 * (m % 2)).wait_recv()
            got_wide(m, 2).wait_recv()

        for jj in range(2):
            for t in range(BAND):
                high, low = halves(a2f[m, jj, t])
                a2s[2 * m + jj, 0:BS, t * BS:(t + 1) * BS] = high
                a2s[2 * m + jj, BS:2 * BS, t * BS:(t + 1) * BS] = low

    def own_step(b, e, m):
        @pl.when(base + m != c)
        def _():
            got_in(b, e, m).wait_recv()

        share_copy(b, e, m).start()

        @pl.when(has_side)
        def _():
            side_copy(b, e, m).start()

        split_block(e, 8 + 2 * m + b)

    def neighbour_step(b, e, m):
        got_share(b, e, m).wait_recv()
        split_block(e, 16 - 16 * core + 2 * m + b)

        @pl.when(has_side)
        def _():
            got_side(b, e, m).wait_recv()
            split_block(e, 16 * core + 2 * m + b)

    def second(e, m):
        for jj in range(2):
            ids = [jnp.clip(bands[m, jj, t] - 2 * base + REACH, 0, 23) for t in range(BAND)]
            res[e, m, jj] = product(a2s[2 * m + jj], [gh[e, k] for k in ids], [gl[e, k] for k in ids])

        @pl.when(base + m != c)
        def _():
            back_copy(e, m).start()

    each(4, far_step)
    each(4, lambda m: relay_step(m, 2))
    for e in range(2):
        each(4, lambda m: own_step(0, e, m))
    to_scalars.wait()

    @pl.when(local_owner)
    def _():
        load_a2.wait()

    each(4, lambda m: own_step(1, 0, m))
    each(4, lambda m: relay_step(m, 0))
    each(2, lambda n: slab_step(2 * near + n))
    for b in range(2):
        each(4, lambda m: neighbour_step(b, 0, m))
    each(2, lambda n: second(0, 2 * near + n))
    each(4, lambda m: own_step(1, 1, m))
    each(2, lambda n: slab_step(2 - 2 * near + n))
    each(2, lambda n: second(0, 2 - 2 * near + n))
    for b in range(2):
        each(4, lambda m: neighbour_step(b, 1, m))
    each(2, lambda n: second(1, 2 * near + n))
    each(2, lambda n: second(1, 2 - 2 * near + n))

    for e in range(2):
        def finish(hp, e=e):
            columns = pl.ds(pl.multiple_of((2 * hp + e) * BS, BS), BS)
            here = both(hp == h, local_owner)

            @pl.when(jnp.logical_not(here))
            def _():
                got_back(e, hp).wait_recv()
                for jj in range(2):
                    out_ref[jj * BS:(jj + 1) * BS, columns] = resin[e, hp, jj]

            @pl.when(here)
            def _():
                for jj in range(2):
                    out_ref[jj * BS:(jj + 1) * BS, columns] = res[e, mine, jj]

        each(4, finish)

    slab_out.wait_send()

    @pl.when(jnp.logical_not(local_owner))
    def _():
        slab_to_mate_core.wait_send()

    def drain_halo(k):
        for b in range(2):
            send_own(b, k).wait_send()

            @pl.when(has_far_to)
            def _():
                send_far(b, k).wait_send()

    each(4, drain_halo)

    def drain(m):
        d, from_origin, from_mate = chain_conds(m)

        @pl.when(from_origin)
        def _():
            chain_copy(m, 0).wait_send()

        @pl.when(from_mate)
        def _():
            chain_copy(m, 1).wait_send()

        @pl.when(d != 0)
        def _():
            for o in (1, 3):
                wide_copy(m, o).wait_send()
            relay_copy(m).wait_send()

        @pl.when(is_remote(m))
        def _():
            band_copy(m).wait_send()
            for e in range(2):
                for b in range(2):
                    in_copy(b, e, m).wait_send()

        for e in range(2):
            for b in range(2):
                share_copy(b, e, m).wait_send()

                @pl.when(has_side)
                def _():
                    side_copy(b, e, m).wait_send()

            @pl.when(base + m != c)
            def _():
                back_copy(e, m).wait_send()

    each(4, drain)


def solution(mesh):
    rows, cols = mesh.shape["row"], mesh.shape["col"]

    def body(state_cov, trans_first, band_first, trans_second, band_second, noise_cov):
        width = state_cov.shape[1]
        tiles = state_cov.reshape(8, BS, width)
        f32, bf16, i32 = jnp.float32, jnp.bfloat16, jnp.int32
        smem = pl.BlockSpec(memory_space=pltpu.SMEM)
        anyspace = pl.BlockSpec(memory_space=pl.ANY)
        dma = pltpu.SemaphoreType.DMA
        product_t = pl.pallas_call(
            lambda *refs: kernel(rows, cols, *refs),
            out_shape=jax.ShapeDtypeStruct((width, 8 * BS), f32),
            in_specs=[smem, smem, anyspace, anyspace, anyspace],
            out_specs=pl.BlockSpec(memory_space=pltpu.VMEM),
            scratch_shapes=[
                pltpu.VMEM((2, 24, BS, BS), f32),
                pltpu.VMEM((2, 24, BS, BS), bf16),
                pltpu.VMEM((2, 24, BS, BS), bf16),
                pltpu.VMEM((8, BAND, BS, BS), f32),
                pltpu.VMEM((8, 2 * BS, BAND * BS), bf16),
                pltpu.VMEM((4, 2, BAND, BS, BS), f32),
                pltpu.VMEM((8, 2 * BS, BAND * BS), bf16),
                pltpu.VMEM((2, 4, 2, BS, BS), f32),
                pltpu.VMEM((24, BS, BS), f32),
                pltpu.VMEM((24, BS, BS), f32),
                pltpu.VMEM((2, 24, BS, BS), bf16),
                pltpu.VMEM((2, 24, BS, BS), bf16),
                pltpu.VMEM((2, 4, 2, BS, BS), f32),
                pltpu.VMEM((2, 4, 2, BS, BS), f32),
                pltpu.VMEM((8, BS), i32),
                pltpu.VMEM((4, 8, BS), i32),
                pltpu.SMEM((4, 8, BS), i32),
                dma((2, 4)), dma((2, 4)), dma((2, 4)), dma((2, 4)),
                dma((2,)), dma((4,)), dma((4,)), dma((4, 3)), dma((4, 3)),
                dma((4,)), dma((4,)), dma((2, 2, 4)), dma((2, 2, 4)),
                dma((2, 2, 4)), dma((2, 2, 4)), dma((2, 2, 4)), dma((2, 2, 4)),
                dma((2, 4)), dma((2, 4)), dma((5,)),
            ],
            compiler_params=pltpu.CompilerParams(
                collective_id=0, has_side_effects=True, vmem_limit_bytes=52 * 2**20
            ),
            name="forecast",
        )(band_first, band_second, tiles, trans_first, trans_second)
        return product_t + noise_cov

    return jax.shard_map(
        body,
        mesh=mesh,
        in_specs=(
            P("row", "col"),
            P("row", None, None, None),
            P("row", None),
            P("col", None, None, None),
            P("col", None),
            P("col", "row"),
        ),
        out_specs=P("col", "row"),
        check_vma=False,
    )
```

```python
import jax
import jax.numpy as jnp
from jax import lax
from jax.experimental import pallas as pl
from jax.experimental.pallas import tpu as pltpu
from jax.sharding import PartitionSpec as P

BAND = 9
REACH = 8
BS = 128
MESH = pl.DeviceIdType.MESH


def halves(x):
    high = x.astype(jnp.bfloat16)
    low = (x - high.astype(jnp.float32)).astype(jnp.bfloat16)
    return high, low


def dot(a, b):
    return jnp.dot(a, b, preferred_element_type=jnp.float32)


def product(a, xs_high, xs_low):
    top = dot(a, jnp.concatenate(xs_high, axis=0))
    return top[:BS] + top[BS:] + dot(a[:BS], jnp.concatenate(xs_low, axis=0))


def each(n, body):
    def step(k, carry):
        body(k)
        return carry
    lax.fori_loop(0, n, step, 0)


def remote(src, dst, send, recv, device):
    return pltpu.make_async_remote_copy(
        src_ref=src, dst_ref=dst, send_sem=send, recv_sem=recv,
        device_id=device, device_id_type=MESH,
    )


def both(*conds):
    out = conds[0]
    for cond in conds[1:]:
        out = jnp.logical_and(out, cond)
    return out


def either(*conds):
    out = conds[0]
    for cond in conds[1:]:
        out = jnp.logical_or(out, cond)
    return out


def kernel(
    rows, cols,
    band1, band2, s_ref, a1_ref, a2_ref, out_ref,
    hb, hbh, hbl, a1f, a1s, a2f, a2s, stage, g0, g1, gh, gl, res, resin, band_mine, band_all, bands,
    own_send, direct_recv, far_send, far_recv,
    slab_send, slab_recv, chain_send, wide_send, wide_recv,
    band_send, band_recv, in_send, in_recv, share_send, share_recv, side_send, side_recv,
    back_send, back_recv, local_sem,
):
    r = lax.axis_index("row")
    c = lax.axis_index("col")
    y = c // 8
    q = c % 8
    h = q // 2
    core = q % 2
    owner = h // 2
    mine = q % 4
    base = 8 * y + 4 * core
    local_owner = core == owner
    x = r // 2
    p = r % 2
    mate = r + 1 - 2 * p
    other = c + 1 - 2 * core
    far_to = r + 2 - 4 * p
    far_from = r - 2 + 4 * p
    has_far_to = both(far_to >= 0, far_to < rows)
    has_far_from = both(far_from >= 0, far_from < rows)
    side = c - 7 + 14 * core
    has_side = both(side >= 0, side < cols)
    out_row = r + 1 - 2 * p
    out_h = (h + 3 + 2 * p) % 4

    def half(b):
        return slice(b * BS, (b + 1) * BS)

    loads_own = [
        pltpu.make_async_copy(s_ref.at[:, :, half(b)], hb.at[b, pl.ds(8, 8)], local_sem.at[b]) for b in range(2)
    ]
    load_a1 = pltpu.make_async_copy(a1_ref, a1f, local_sem.at[2])
    load_a2 = pltpu.make_async_copy(a2_ref, a2f.at[mine], local_sem.at[3])
    loads_own[0].start()
    load_a1.start()
    loads_own[1].start()

    @pl.when(local_owner)
    def _():
        load_a2.start()

    barrier = pltpu.get_barrier_semaphore()

    def greet(device):
        pl.semaphore_signal(barrier, inc=1, device_id=device, device_id_type=MESH)

    for o in range(1, 8):
        greet((r, 8 * y + (q + o) % 8))
    for o in range(1, rows // 2):
        greet(((r + 2 * o) % rows, c))
    for k in range(2):
        greet((mate, 8 * y + 2 * h + k))
        greet((out_row, 8 * y + 2 * out_h + k))

    @pl.when(has_side)
    def _():
        greet((r, side))

    pl.semaphore_wait(barrier, 7 + rows // 2 - 1 + 4 + has_side.astype(jnp.int32))

    near_at = 16 - 16 * p
    away_at = 16 * p

    def send_own(b, k):
        return remote(
            s_ref.at[pl.ds(2 * k, 2), :, half(b)], hb.at[b, pl.ds(16 * p + 2 * k, 2)],
            own_send.at[b, k], direct_recv.at[b, k], (mate, c),
        )

    def send_far(b, k):
        return remote(
            hb.at[b, pl.ds(near_at + 2 * k, 2)], hb.at[b, pl.ds(16 * p + 2 * k, 2)],
            far_send.at[b, k], far_recv.at[b, k], (far_to, c),
        )

    def got_direct(b, k):
        at = hb.at[b, pl.ds(near_at + 2 * k, 2)]
        return remote(at, at, own_send.at[b, k], direct_recv.at[b, k], (mate, c))

    def got_far(b, k):
        at = hb.at[b, pl.ds(away_at + 2 * k, 2)]
        return remote(at, at, far_send.at[b, k], far_recv.at[b, k], (mate, c))

    each(4, lambda k: send_own(0, k).start())

    part = BS // (rows // 2)

    def piece(m, at):
        return a2f.at[m, :, :, pl.ds(pl.multiple_of(part * at, part), part), :]

    slab_to_mate_core = remote(a2_ref, a2f.at[mine], slab_send.at[0], slab_recv.at[mine], (r, other))
    slab_out = remote(
        a2_ref.at[:, :, pl.ds(pl.multiple_of(part * x, part), part), :], piece(mine, x),
        slab_send.at[1], slab_recv.at[mine], (out_row, 8 * y + 2 * out_h + owner),
    )
    slab_out.start()

    @pl.when(jnp.logical_not(local_owner))
    def _():
        slab_to_mate_core.start()

    def far_of(m):
        return (2 * core + m // 2 - h + 4) % 4

    def chain_conds(m):
        d = far_of(m)
        from_origin = either(both(d == 3, p == 0), both(d == 1, p == 1))
        from_mate = either(both(d == 3, p == 1), both(d == 1, p == 0))
        return d, from_origin, from_mate

    def chain_copy(m, way):
        device = (mate, c) if way == 0 else (out_row, 8 * y + 2 * out_h + core)
        return remote(piece(m, x), piece(m, x), chain_send.at[m], slab_recv.at[m], device)

    def wide_copy(m, o):
        return remote(piece(m, x), piece(m, x), wide_send.at[m, o - 1], wide_recv.at[m, o - 1], ((r + 2 * o) % rows, c))

    def got_wide(m, o):
        at = (x - o + rows // 2) % (rows // 2)
        return remote(piece(m, x), piece(m, at), wide_send.at[m, o - 1], wide_recv.at[m, o - 1], (mate, c))

    def relay_copy(m):
        odd = m % 2
        at = (x + 3 - 2 * odd) % 4
        return remote(
            piece(m, at), piece(m, at), wide_send.at[m, 1], wide_recv.at[m, 1], ((r + 2 - 4 * odd + rows) % rows, c)
        )

    def widen(m):
        for o in (1, 3):
            wide_copy(m, o).start()

    def relay(m):
        got_wide(m, 1 + 2 * (m % 2)).wait_recv()
        relay_copy(m).start()

    def relay_step(m, kind):
        cond = far_of(m) == 2 if kind == 0 else chain_conds(m)[kind]

        @pl.when(cond)
        def _():
            relay(m)

    def origin_step(m):
        @pl.when(chain_conds(m)[1])
        def _():
            chain_copy(m, 0).wait_recv()
            chain_copy(m, 0).start()

    def origin_widen(m):
        @pl.when(chain_conds(m)[1])
        def _():
            widen(m)

    def mate_step(m):
        @pl.when(chain_conds(m)[2])
        def _():
            chain_copy(m, 1).wait_recv()
            chain_copy(m, 1).start()

    def mate_widen(m):
        @pl.when(chain_conds(m)[2])
        def _():
            widen(m)

    def far_step(m):
        @pl.when(far_of(m) == 2)
        def _():
            chain_copy(m, 0).wait_recv()
            widen(m)

    row_id = lax.broadcasted_iota(jnp.int32, (8, BS), 0)
    lane_id = lax.broadcasted_iota(jnp.int32, (8, BS), 1)
    table = jnp.zeros((8, BS), jnp.int32)
    for j in range(2):
        for t in range(BAND):
            table = jnp.where(both(row_id == j, lane_id == t), band2[j, t], table)
    band_mine[...] = table

    @pl.when(local_owner)
    def _():
        band_all[mine] = table

    def group_copy(src, dst, send, recv, o):
        return remote(src, dst, send, recv, (r, 8 * y + 2 * ((h + o) % 4) + owner))

    def band_copy(o):
        return group_copy(band_mine, band_all.at[mine], band_send.at[o], band_recv.at[mine], o)

    def got_band(m):
        return remote(band_mine, band_all.at[m], band_send.at[0], band_recv.at[m], (mate, c))

    def is_remote(o):
        return jnp.logical_or(o != 0, jnp.logical_not(local_owner))

    for o in range(4):
        @pl.when(is_remote(o))
        def _():
            band_copy(o).start()

    loads_own[0].wait()
    load_a1.wait()

    def split_rows(b, at):
        for n in range(2):
            high, low = halves(hb[b, at + n])
            hbh[b, at + n] = high
            hbl[b, at + n] = low

    def split_first(i):
        for t in range(BAND):
            high, low = halves(a1f[i, t])
            a1s[i, 0:BS, t * BS:(t + 1) * BS] = high
            a1s[i, BS:2 * BS, t * BS:(t + 1) * BS] = low

    def direct_step(b, k):
        split_rows(b, 8 + 2 * k)
        got_direct(b, k).wait_recv()

        @pl.when(has_far_to)
        def _():
            send_far(b, k).start()

        split_rows(b, near_at + 2 * k)

    def away_step(b, k):
        @pl.when(has_far_from)
        def _():
            got_far(b, k).wait_recv()
            split_rows(b, away_at + 2 * k)

    gs = (g0, g1)

    def in_copy(b, e, o):
        hp = (h + o) % 4
        return group_copy(
            stage.at[e, hp, b], gs[e].at[8 + 2 * mine + b], in_send.at[b, e, o], in_recv.at[b, e, mine], o
        )

    def got_in(b, e, m):
        at = gs[e].at[8 + 2 * m + b]
        return remote(at, at, in_send.at[b, e, 0], in_recv.at[b, e, m], (mate, c))

    def advect(b, e, n):
        o = 3 - n
        hp = (h + o) % 4
        i = 2 * hp + e
        ids = [jnp.clip(band1[i, t] - 8 * r + REACH, 0, 23) for t in range(BAND)]
        tile = product(a1s[i], [hbh[b, k] for k in ids], [hbl[b, k] for k in ids]).T
        stage[e, hp, b] = tile

        @pl.when(is_remote(o))
        def _():
            in_copy(b, e, o).start()

        @pl.when(jnp.logical_not(is_remote(o)))
        def _():
            gs[e][8 + 2 * mine + b] = tile

    def first_step(k):
        for n in range(2):
            split_first(2 * k + n)
        direct_step(0, k)

    each(3, first_step)
    each(4, origin_step)
    each(4, lambda k: send_own(1, k).start())
    first_step(3)
    each(4, origin_widen)
    loads_own[1].wait()
    each(4, lambda k: away_step(0, k))
    each(4, mate_step)
    each(4, lambda n: advect(0, 0, n))
    each(4, lambda n: advect(0, 1, n))
    each(4, lambda k: direct_step(1, k))
    each(4, mate_widen)
    each(4, lambda m: relay_step(m, 1))
    each(4, lambda k: away_step(1, k))
    each(4, lambda n: advect(1, 0, n))
    each(4, far_step)
    each(4, lambda n: advect(1, 1, n))

    for m in range(4):
        @pl.when(base + m != c)
        def _():
            got_band(m).wait_recv()
    to_scalars = pltpu.make_async_copy(band_all, bands, local_sem.at[4])
    to_scalars.start()

    def share_copy(b, e, m):
        return remote(
            gs[e].at[8 + 2 * m + b], gs[e].at[16 * core + 2 * m + b],
            share_send.at[b, e, m], share_recv.at[b, e, m], (r, other),
        )

    def side_copy(b, e, m):
        return remote(
            gs[e].at[8 + 2 * m + b], gs[e].at[16 - 16 * core + 2 * m + b],
            side_send.at[b, e, m], side_recv.at[b, e, m], (r, side),
        )

    def got_share(b, e, m):
        at = gs[e].at[16 - 16 * core + 2 * m + b]
        return remote(at, at, share_send.at[b, e, m], share_recv.at[b, e, m], (r, other))

    def got_side(b, e, m):
        at = gs[e].at[16 * core + 2 * m + b]
        return remote(at, at, side_send.at[b, e, m], side_recv.at[b, e, m], (r, other))

    def back_copy(e, m):
        return remote(res.at[e, m], resin.at[e, h], back_send.at[e, m], back_recv.at[e, h], (r, base + m))

    def got_back(e, hp):
        return remote(res.at[e, 0], resin.at[e, hp], back_send.at[e, 0], back_recv.at[e, hp], (mate, c))

    def split_block(e, at):
        high, low = halves(gs[e][at])
        gh[e, at] = high
        gl[e, at] = low

    near = jnp.where(local_owner, h % 2, 1 - h % 2)

    def slab_step(m):
        @pl.when(both(far_of(m) == 0, base + m != c))
        def _():
            remote(a2_ref, a2f.at[m], slab_send.at[0], slab_recv.at[m], (r, other)).wait_recv()

        @pl.when(far_of(m) != 0)
        def _():
            got_wide(m, 3 - 2 * (m % 2)).wait_recv()
            got_wide(m, 2).wait_recv()

        for jj in range(2):
            for t in range(BAND):
                high, low = halves(a2f[m, jj, t])
                a2s[2 * m + jj, 0:BS, t * BS:(t + 1) * BS] = high
                a2s[2 * m + jj, BS:2 * BS, t * BS:(t + 1) * BS] = low

    def own_step(b, e, m):
        @pl.when(base + m != c)
        def _():
            got_in(b, e, m).wait_recv()

        share_copy(b, e, m).start()

        @pl.when(has_side)
        def _():
            side_copy(b, e, m).start()

        split_block(e, 8 + 2 * m + b)

    def neighbour_step(b, e, m):
        got_share(b, e, m).wait_recv()
        split_block(e, 16 - 16 * core + 2 * m + b)

        @pl.when(has_side)
        def _():
            got_side(b, e, m).wait_recv()
            split_block(e, 16 * core + 2 * m + b)

    def second(e, m):
        for jj in range(2):
            ids = [jnp.clip(bands[m, jj, t] - 2 * base + REACH, 0, 23) for t in range(BAND)]
            res[e, m, jj] = product(a2s[2 * m + jj], [gh[e, k] for k in ids], [gl[e, k] for k in ids])

        @pl.when(base + m != c)
        def _():
            back_copy(e, m).start()

    each(4, lambda m: relay_step(m, 2))
    for e in range(2):
        each(4, lambda m: own_step(0, e, m))
    to_scalars.wait()

    @pl.when(local_owner)
    def _():
        load_a2.wait()

    each(4, lambda m: own_step(1, 0, m))
    each(4, lambda m: relay_step(m, 0))
    each(2, lambda n: slab_step(2 * near + n))
    for b in range(2):
        each(4, lambda m: neighbour_step(b, 0, m))
    each(2, lambda n: second(0, 2 * near + n))
    each(4, lambda m: own_step(1, 1, m))
    each(2, lambda n: slab_step(2 - 2 * near + n))
    each(2, lambda n: second(0, 2 - 2 * near + n))
    for b in range(2):
        each(4, lambda m: neighbour_step(b, 1, m))
    each(2, lambda n: second(1, 2 * near + n))
    each(2, lambda n: second(1, 2 - 2 * near + n))

    for e in range(2):
        def finish(hp, e=e):
            columns = pl.ds(pl.multiple_of((2 * hp + e) * BS, BS), BS)
            here = both(hp == h, local_owner)

            @pl.when(jnp.logical_not(here))
            def _():
                got_back(e, hp).wait_recv()
                for jj in range(2):
                    out_ref[jj * BS:(jj + 1) * BS, columns] = resin[e, hp, jj]

            @pl.when(here)
            def _():
                for jj in range(2):
                    out_ref[jj * BS:(jj + 1) * BS, columns] = res[e, mine, jj]

        each(4, finish)

    slab_out.wait_send()

    @pl.when(jnp.logical_not(local_owner))
    def _():
        slab_to_mate_core.wait_send()

    def drain_halo(k):
        for b in range(2):
            send_own(b, k).wait_send()

            @pl.when(has_far_to)
            def _():
                send_far(b, k).wait_send()

    each(4, drain_halo)

    def drain(m):
        d, from_origin, from_mate = chain_conds(m)

        @pl.when(from_origin)
        def _():
            chain_copy(m, 0).wait_send()

        @pl.when(from_mate)
        def _():
            chain_copy(m, 1).wait_send()

        @pl.when(d != 0)
        def _():
            for o in (1, 3):
                wide_copy(m, o).wait_send()
            relay_copy(m).wait_send()

        @pl.when(is_remote(m))
        def _():
            band_copy(m).wait_send()
            for e in range(2):
                for b in range(2):
                    in_copy(b, e, m).wait_send()

        for e in range(2):
            for b in range(2):
                share_copy(b, e, m).wait_send()

                @pl.when(has_side)
                def _():
                    side_copy(b, e, m).wait_send()

            @pl.when(base + m != c)
            def _():
                back_copy(e, m).wait_send()

    each(4, drain)


def solution(mesh):
    rows, cols = mesh.shape["row"], mesh.shape["col"]

    def body(state_cov, trans_first, band_first, trans_second, band_second, noise_cov):
        width = state_cov.shape[1]
        tiles = state_cov.reshape(8, BS, width)
        f32, bf16, i32 = jnp.float32, jnp.bfloat16, jnp.int32
        smem = pl.BlockSpec(memory_space=pltpu.SMEM)
        anyspace = pl.BlockSpec(memory_space=pl.ANY)
        dma = pltpu.SemaphoreType.DMA
        product_t = pl.pallas_call(
            lambda *refs: kernel(rows, cols, *refs),
            out_shape=jax.ShapeDtypeStruct((width, 8 * BS), f32),
            in_specs=[smem, smem, anyspace, anyspace, anyspace],
            out_specs=pl.BlockSpec(memory_space=pltpu.VMEM),
            scratch_shapes=[
                pltpu.VMEM((2, 24, BS, BS), f32),
                pltpu.VMEM((2, 24, BS, BS), bf16),
                pltpu.VMEM((2, 24, BS, BS), bf16),
                pltpu.VMEM((8, BAND, BS, BS), f32),
                pltpu.VMEM((8, 2 * BS, BAND * BS), bf16),
                pltpu.VMEM((4, 2, BAND, BS, BS), f32),
                pltpu.VMEM((8, 2 * BS, BAND * BS), bf16),
                pltpu.VMEM((2, 4, 2, BS, BS), f32),
                pltpu.VMEM((24, BS, BS), f32),
                pltpu.VMEM((24, BS, BS), f32),
                pltpu.VMEM((2, 24, BS, BS), bf16),
                pltpu.VMEM((2, 24, BS, BS), bf16),
                pltpu.VMEM((2, 4, 2, BS, BS), f32),
                pltpu.VMEM((2, 4, 2, BS, BS), f32),
                pltpu.VMEM((8, BS), i32),
                pltpu.VMEM((4, 8, BS), i32),
                pltpu.SMEM((4, 8, BS), i32),
                dma((2, 4)), dma((2, 4)), dma((2, 4)), dma((2, 4)),
                dma((2,)), dma((4,)), dma((4,)), dma((4, 3)), dma((4, 3)),
                dma((4,)), dma((4,)), dma((2, 2, 4)), dma((2, 2, 4)),
                dma((2, 2, 4)), dma((2, 2, 4)), dma((2, 2, 4)), dma((2, 2, 4)),
                dma((2, 4)), dma((2, 4)), dma((5,)),
            ],
            compiler_params=pltpu.CompilerParams(
                collective_id=0, has_side_effects=True, vmem_limit_bytes=52 * 2**20
            ),
            name="forecast",
        )(band_first, band_second, tiles, trans_first, trans_second)
        return product_t + noise_cov

    return jax.shard_map(
        body,
        mesh=mesh,
        in_specs=(
            P("row", "col"),
            P("row", None, None, None),
            P("row", None),
            P("col", None, None, None),
            P("col", None),
            P("col", "row"),
        ),
        out_specs=P("col", "row"),
        check_vma=False,
    )
```

```python
import jax
import jax.numpy as jnp
from jax import lax
from jax.experimental import pallas as pl
from jax.experimental.pallas import tpu as pltpu
from jax.sharding import PartitionSpec as P

BAND = 9
REACH = 8
BS = 128
MESH = pl.DeviceIdType.MESH


def halves(x):
    high = x.astype(jnp.bfloat16)
    low = (x - high.astype(jnp.float32)).astype(jnp.bfloat16)
    return high, low


def dot(a, b):
    return jnp.dot(a, b, preferred_element_type=jnp.float32)


def product(a, xs_high, xs_low):
    top = dot(a, jnp.concatenate(xs_high, axis=0))
    return top[:BS] + top[BS:] + dot(a[:BS], jnp.concatenate(xs_low, axis=0))


def each(n, body):
    def step(k, carry):
        body(k)
        return carry
    lax.fori_loop(0, n, step, 0)


def remote(src, dst, send, recv, device):
    return pltpu.make_async_remote_copy(
        src_ref=src, dst_ref=dst, send_sem=send, recv_sem=recv,
        device_id=device, device_id_type=MESH,
    )


def both(*conds):
    out = conds[0]
    for cond in conds[1:]:
        out = jnp.logical_and(out, cond)
    return out


def either(*conds):
    out = conds[0]
    for cond in conds[1:]:
        out = jnp.logical_or(out, cond)
    return out


def kernel(
    rows, cols,
    band1, band2, s_ref, a1_ref, a2_ref, out_ref,
    hb, hbh, hbl, a1f, a1s, a2f, a2s, stage, g0, g1, gh, gl, res, resin, band_mine, band_all, bands,
    own_send, direct_recv, far_send, far_recv,
    slab_send, slab_recv, chain_send, wide_send, wide_recv,
    band_send, band_recv, in_send, in_recv, share_send, share_recv, side_send, side_recv,
    back_send, back_recv, local_sem,
):
    r = lax.axis_index("row")
    c = lax.axis_index("col")
    y = c // 8
    q = c % 8
    h = q // 2
    core = q % 2
    owner = h // 2
    mine = q % 4
    base = 8 * y + 4 * core
    local_owner = core == owner
    x = r // 2
    p = r % 2
    mate = r + 1 - 2 * p
    other = c + 1 - 2 * core
    far_to = r + 2 - 4 * p
    far_from = r - 2 + 4 * p
    has_far_to = both(far_to >= 0, far_to < rows)
    has_far_from = both(far_from >= 0, far_from < rows)
    side = c - 7 + 14 * core
    has_side = both(side >= 0, side < cols)
    out_row = r + 1 - 2 * p
    out_h = (h + 3 + 2 * p) % 4

    def half(b):
        return slice(b * BS, (b + 1) * BS)

    loads_own = [
        pltpu.make_async_copy(s_ref.at[:, :, half(b)], hb.at[b, pl.ds(8, 8)], local_sem.at[b]) for b in range(2)
    ]
    load_a1 = pltpu.make_async_copy(a1_ref, a1f, local_sem.at[2])
    load_a2 = pltpu.make_async_copy(a2_ref, a2f.at[mine], local_sem.at[3])
    loads_own[0].start()
    load_a1.start()
    loads_own[1].start()

    @pl.when(local_owner)
    def _():
        load_a2.start()

    barrier = pltpu.get_barrier_semaphore()

    def greet(device):
        pl.semaphore_signal(barrier, inc=1, device_id=device, device_id_type=MESH)

    for o in range(1, 8):
        greet((r, 8 * y + (q + o) % 8))
    for o in range(1, rows // 2):
        greet(((r + 2 * o) % rows, c))
    for k in range(2):
        greet((mate, 8 * y + 2 * h + k))
        greet((out_row, 8 * y + 2 * out_h + k))

    @pl.when(has_side)
    def _():
        greet((r, side))

    pl.semaphore_wait(barrier, 7 + rows // 2 - 1 + 4 + has_side.astype(jnp.int32))

    near_at = 16 - 16 * p
    away_at = 16 * p

    def send_own(b, k):
        return remote(
            s_ref.at[pl.ds(2 * k, 2), :, half(b)], hb.at[b, pl.ds(16 * p + 2 * k, 2)],
            own_send.at[b, k], direct_recv.at[b, k], (mate, c),
        )

    def send_far(b, k):
        return remote(
            hb.at[b, pl.ds(near_at + 2 * k, 2)], hb.at[b, pl.ds(16 * p + 2 * k, 2)],
            far_send.at[b, k], far_recv.at[b, k], (far_to, c),
        )

    def got_direct(b, k):
        at = hb.at[b, pl.ds(near_at + 2 * k, 2)]
        return remote(at, at, own_send.at[b, k], direct_recv.at[b, k], (mate, c))

    def got_far(b, k):
        at = hb.at[b, pl.ds(away_at + 2 * k, 2)]
        return remote(at, at, far_send.at[b, k], far_recv.at[b, k], (mate, c))

    each(4, lambda k: send_own(0, k).start())

    part = BS // (rows // 2)

    def piece(m, at):
        return a2f.at[m, :, :, pl.ds(pl.multiple_of(part * at, part), part), :]

    slab_to_mate_core = remote(a2_ref, a2f.at[mine], slab_send.at[0], slab_recv.at[mine], (r, other))
    slab_out = remote(
        a2_ref.at[:, :, pl.ds(pl.multiple_of(part * x, part), part), :], piece(mine, x),
        slab_send.at[1], slab_recv.at[mine], (out_row, 8 * y + 2 * out_h + owner),
    )
    slab_out.start()

    @pl.when(jnp.logical_not(local_owner))
    def _():
        slab_to_mate_core.start()

    def far_of(m):
        return (2 * core + m // 2 - h + 4) % 4

    def chain_conds(m):
        d = far_of(m)
        from_origin = either(both(d == 3, p == 0), both(d == 1, p == 1))
        from_mate = either(both(d == 3, p == 1), both(d == 1, p == 0))
        return d, from_origin, from_mate

    def chain_copy(m, way):
        device = (mate, c) if way == 0 else (out_row, 8 * y + 2 * out_h + core)
        return remote(piece(m, x), piece(m, x), chain_send.at[m], slab_recv.at[m], device)

    def wide_copy(m, o):
        return remote(piece(m, x), piece(m, x), wide_send.at[m, o - 1], wide_recv.at[m, o - 1], ((r + 2 * o) % rows, c))

    def got_wide(m, o):
        at = (x - o + rows // 2) % (rows // 2)
        return remote(piece(m, x), piece(m, at), wide_send.at[m, o - 1], wide_recv.at[m, o - 1], (mate, c))

    def relay_copy(m):
        odd = m % 2
        at = (x + 3 - 2 * odd) % 4
        return remote(
            piece(m, at), piece(m, at), wide_send.at[m, 1], wide_recv.at[m, 1], ((r + 2 - 4 * odd + rows) % rows, c)
        )

    def widen(m):
        for o in (1, 3):
            wide_copy(m, o).start()

    def relay(m):
        got_wide(m, 1 + 2 * (m % 2)).wait_recv()
        relay_copy(m).start()

    def relay_step(m, kind):
        cond = far_of(m) == 2 if kind == 0 else chain_conds(m)[kind]

        @pl.when(cond)
        def _():
            relay(m)

    def origin_step(m):
        @pl.when(chain_conds(m)[1])
        def _():
            chain_copy(m, 0).wait_recv()
            chain_copy(m, 0).start()

    def origin_widen(m):
        @pl.when(chain_conds(m)[1])
        def _():
            widen(m)

    def mate_step(m):
        @pl.when(chain_conds(m)[2])
        def _():
            chain_copy(m, 1).wait_recv()
            chain_copy(m, 1).start()

    def mate_widen(m):
        @pl.when(chain_conds(m)[2])
        def _():
            widen(m)

    def far_step(m):
        @pl.when(far_of(m) == 2)
        def _():
            chain_copy(m, 0).wait_recv()
            widen(m)

    row_id = lax.broadcasted_iota(jnp.int32, (8, BS), 0)
    lane_id = lax.broadcasted_iota(jnp.int32, (8, BS), 1)
    table = jnp.zeros((8, BS), jnp.int32)
    for j in range(2):
        for t in range(BAND):
            table = jnp.where(both(row_id == j, lane_id == t), band2[j, t], table)
    band_mine[...] = table

    @pl.when(local_owner)
    def _():
        band_all[mine] = table

    def group_copy(src, dst, send, recv, o):
        return remote(src, dst, send, recv, (r, 8 * y + 2 * ((h + o) % 4) + owner))

    def band_copy(o):
        return group_copy(band_mine, band_all.at[mine], band_send.at[o], band_recv.at[mine], o)

    def got_band(m):
        return remote(band_mine, band_all.at[m], band_send.at[0], band_recv.at[m], (mate, c))

    def is_remote(o):
        return jnp.logical_or(o != 0, jnp.logical_not(local_owner))

    for o in range(4):
        @pl.when(is_remote(o))
        def _():
            band_copy(o).start()

    loads_own[0].wait()
    load_a1.wait()

    def split_rows(b, at):
        for n in range(2):
            high, low = halves(hb[b, at + n])
            hbh[b, at + n] = high
            hbl[b, at + n] = low

    def split_first(i):
        for t in range(BAND):
            high, low = halves(a1f[i, t])
            a1s[i, 0:BS, t * BS:(t + 1) * BS] = high
            a1s[i, BS:2 * BS, t * BS:(t + 1) * BS] = low

    def direct_step(b, k):
        split_rows(b, 8 + 2 * k)
        got_direct(b, k).wait_recv()

        @pl.when(has_far_to)
        def _():
            send_far(b, k).start()

        split_rows(b, near_at + 2 * k)

    def away_step(b, k):
        @pl.when(has_far_from)
        def _():
            got_far(b, k).wait_recv()
            split_rows(b, away_at + 2 * k)

    gs = (g0, g1)

    def in_copy(b, e, o):
        hp = (h + o) % 4
        return group_copy(
            stage.at[e, hp, b], gs[e].at[8 + 2 * mine + b], in_send.at[b, e, o], in_recv.at[b, e, mine], o
        )

    def got_in(b, e, m):
        at = gs[e].at[8 + 2 * m + b]
        return remote(at, at, in_send.at[b, e, 0], in_recv.at[b, e, m], (mate, c))

    def advect(b, e, n):
        o = 3 - n
        hp = (h + o) % 4
        i = 2 * hp + e
        ids = [jnp.clip(band1[i, t] - 8 * r + REACH, 0, 23) for t in range(BAND)]
        tile = product(a1s[i], [hbh[b, k] for k in ids], [hbl[b, k] for k in ids]).T
        stage[e, hp, b] = tile

        @pl.when(is_remote(o))
        def _():
            in_copy(b, e, o).start()

        @pl.when(jnp.logical_not(is_remote(o)))
        def _():
            gs[e][8 + 2 * mine + b] = tile

    def first_step(k):
        for n in range(2):
            split_first(2 * k + n)
        direct_step(0, k)

    each(3, first_step)
    each(4, origin_step)
    each(4, lambda k: send_own(1, k).start())
    first_step(3)
    each(4, origin_widen)
    loads_own[1].wait()
    each(4, lambda k: away_step(0, k))
    each(4, mate_step)
    each(4, lambda n: advect(0, 0, n))
    each(4, lambda n: advect(0, 1, n))
    each(4, lambda k: direct_step(1, k))
    each(4, mate_widen)
    each(4, lambda m: relay_step(m, 1))
    each(4, lambda k: away_step(1, k))
    each(4, lambda n: advect(1, 0, n))
    each(4, far_step)
    each(4, lambda n: advect(1, 1, n))

    for m in range(4):
        @pl.when(base + m != c)
        def _():
            got_band(m).wait_recv()
    to_scalars = pltpu.make_async_copy(band_all, bands, local_sem.at[4])
    to_scalars.start()

    def share_copy(b, e, m):
        return remote(
            gs[e].at[8 + 2 * m + b], gs[e].at[16 * core + 2 * m + b],
            share_send.at[b, e, m], share_recv.at[b, e, m], (r, other),
        )

    def side_copy(b, e, m):
        return remote(
            gs[e].at[8 + 2 * m + b], gs[e].at[16 - 16 * core + 2 * m + b],
            side_send.at[b, e, m], side_recv.at[b, e, m], (r, side),
        )

    def got_share(b, e, m):
        at = gs[e].at[16 - 16 * core + 2 * m + b]
        return remote(at, at, share_send.at[b, e, m], share_recv.at[b, e, m], (r, other))

    def got_side(b, e, m):
        at = gs[e].at[16 * core + 2 * m + b]
        return remote(at, at, side_send.at[b, e, m], side_recv.at[b, e, m], (r, other))

    def back_copy(e, m):
        return remote(res.at[e, m], resin.at[e, h], back_send.at[e, m], back_recv.at[e, h], (r, base + m))

    def got_back(e, hp):
        return remote(res.at[e, 0], resin.at[e, hp], back_send.at[e, 0], back_recv.at[e, hp], (mate, c))

    def split_block(e, at):
        high, low = halves(gs[e][at])
        gh[e, at] = high
        gl[e, at] = low

    near = jnp.where(local_owner, h % 2, 1 - h % 2)

    def slab_step(m):
        @pl.when(both(far_of(m) == 0, base + m != c))
        def _():
            remote(a2_ref, a2f.at[m], slab_send.at[0], slab_recv.at[m], (r, other)).wait_recv()

        @pl.when(far_of(m) != 0)
        def _():
            got_wide(m, 3 - 2 * (m % 2)).wait_recv()
            got_wide(m, 2).wait_recv()

        for jj in range(2):
            for t in range(BAND):
                high, low = halves(a2f[m, jj, t])
                a2s[2 * m + jj, 0:BS, t * BS:(t + 1) * BS] = high
                a2s[2 * m + jj, BS:2 * BS, t * BS:(t + 1) * BS] = low

    def own_step(b, e, m):
        @pl.when(base + m != c)
        def _():
            got_in(b, e, m).wait_recv()

        share_copy(b, e, m).start()

        @pl.when(has_side)
        def _():
            side_copy(b, e, m).start()

        split_block(e, 8 + 2 * m + b)

    def neighbour_step(b, e, m):
        got_share(b, e, m).wait_recv()
        split_block(e, 16 - 16 * core + 2 * m + b)

        @pl.when(has_side)
        def _():
            got_side(b, e, m).wait_recv()
            split_block(e, 16 * core + 2 * m + b)

    def second(e, m):
        for jj in range(2):
            ids = [jnp.clip(bands[m, jj, t] - 2 * base + REACH, 0, 23) for t in range(BAND)]
            res[e, m, jj] = product(a2s[2 * m + jj], [gh[e, k] for k in ids], [gl[e, k] for k in ids])

        @pl.when(base + m != c)
        def _():
            back_copy(e, m).start()

    each(4, lambda m: relay_step(m, 2))
    for e in range(2):
        each(4, lambda m: own_step(0, e, m))
    to_scalars.wait()

    @pl.when(local_owner)
    def _():
        load_a2.wait()

    each(4, lambda m: own_step(1, 0, m))
    each(4, lambda m: relay_step(m, 0))
    each(2, lambda n: slab_step(2 * near + n))
    for b in range(2):
        each(4, lambda m: neighbour_step(b, 0, m))
    each(2, lambda n: second(0, 2 * near + n))
    each(4, lambda m: own_step(1, 1, m))
    each(2, lambda n: slab_step(2 - 2 * near + n))
    each(2, lambda n: second(0, 2 - 2 * near + n))
    for b in range(2):
        each(4, lambda m: neighbour_step(b, 1, m))
    each(2, lambda n: second(1, 2 - 2 * near + n))
    each(2, lambda n: second(1, 2 * near + n))

    for e in range(2):
        def finish(hp, e=e):
            columns = pl.ds(pl.multiple_of((2 * hp + e) * BS, BS), BS)
            here = both(hp == h, local_owner)

            @pl.when(jnp.logical_not(here))
            def _():
                got_back(e, hp).wait_recv()
                for jj in range(2):
                    out_ref[jj * BS:(jj + 1) * BS, columns] = resin[e, hp, jj]

            @pl.when(here)
            def _():
                for jj in range(2):
                    out_ref[jj * BS:(jj + 1) * BS, columns] = res[e, mine, jj]

        each(4, finish)

    slab_out.wait_send()

    @pl.when(jnp.logical_not(local_owner))
    def _():
        slab_to_mate_core.wait_send()

    def drain_halo(k):
        for b in range(2):
            send_own(b, k).wait_send()

            @pl.when(has_far_to)
            def _():
                send_far(b, k).wait_send()

    each(4, drain_halo)

    def drain(m):
        d, from_origin, from_mate = chain_conds(m)

        @pl.when(from_origin)
        def _():
            chain_copy(m, 0).wait_send()

        @pl.when(from_mate)
        def _():
            chain_copy(m, 1).wait_send()

        @pl.when(d != 0)
        def _():
            for o in (1, 3):
                wide_copy(m, o).wait_send()
            relay_copy(m).wait_send()

        @pl.when(is_remote(m))
        def _():
            band_copy(m).wait_send()
            for e in range(2):
                for b in range(2):
                    in_copy(b, e, m).wait_send()

        for e in range(2):
            for b in range(2):
                share_copy(b, e, m).wait_send()

                @pl.when(has_side)
                def _():
                    side_copy(b, e, m).wait_send()

            @pl.when(base + m != c)
            def _():
                back_copy(e, m).wait_send()

    each(4, drain)


def solution(mesh):
    rows, cols = mesh.shape["row"], mesh.shape["col"]

    def body(state_cov, trans_first, band_first, trans_second, band_second, noise_cov):
        width = state_cov.shape[1]
        tiles = state_cov.reshape(8, BS, width)
        f32, bf16, i32 = jnp.float32, jnp.bfloat16, jnp.int32
        smem = pl.BlockSpec(memory_space=pltpu.SMEM)
        anyspace = pl.BlockSpec(memory_space=pl.ANY)
        dma = pltpu.SemaphoreType.DMA
        product_t = pl.pallas_call(
            lambda *refs: kernel(rows, cols, *refs),
            out_shape=jax.ShapeDtypeStruct((width, 8 * BS), f32),
            in_specs=[smem, smem, anyspace, anyspace, anyspace],
            out_specs=pl.BlockSpec(memory_space=pltpu.VMEM),
            scratch_shapes=[
                pltpu.VMEM((2, 24, BS, BS), f32),
                pltpu.VMEM((2, 24, BS, BS), bf16),
                pltpu.VMEM((2, 24, BS, BS), bf16),
                pltpu.VMEM((8, BAND, BS, BS), f32),
                pltpu.VMEM((8, 2 * BS, BAND * BS), bf16),
                pltpu.VMEM((4, 2, BAND, BS, BS), f32),
                pltpu.VMEM((8, 2 * BS, BAND * BS), bf16),
                pltpu.VMEM((2, 4, 2, BS, BS), f32),
                pltpu.VMEM((24, BS, BS), f32),
                pltpu.VMEM((24, BS, BS), f32),
                pltpu.VMEM((2, 24, BS, BS), bf16),
                pltpu.VMEM((2, 24, BS, BS), bf16),
                pltpu.VMEM((2, 4, 2, BS, BS), f32),
                pltpu.VMEM((2, 4, 2, BS, BS), f32),
                pltpu.VMEM((8, BS), i32),
                pltpu.VMEM((4, 8, BS), i32),
                pltpu.SMEM((4, 8, BS), i32),
                dma((2, 4)), dma((2, 4)), dma((2, 4)), dma((2, 4)),
                dma((2,)), dma((4,)), dma((4,)), dma((4, 3)), dma((4, 3)),
                dma((4,)), dma((4,)), dma((2, 2, 4)), dma((2, 2, 4)),
                dma((2, 2, 4)), dma((2, 2, 4)), dma((2, 2, 4)), dma((2, 2, 4)),
                dma((2, 4)), dma((2, 4)), dma((5,)),
            ],
            compiler_params=pltpu.CompilerParams(
                collective_id=0, has_side_effects=True, vmem_limit_bytes=52 * 2**20
            ),
            name="forecast",
        )(band_first, band_second, tiles, trans_first, trans_second)
        return product_t + noise_cov

    return jax.shard_map(
        body,
        mesh=mesh,
        in_specs=(
            P("row", "col"),
            P("row", None, None, None),
            P("row", None),
            P("col", None, None, None),
            P("col", None),
            P("col", "row"),
        ),
        out_specs=P("col", "row"),
        check_vma=False,
    )
```
